512 devices in a mesh: gx: 16 (over z), gy: 32 (over x, y, core).
Axes of the slice: x: 4, y: 4, z: 16, core: 2. Of those that a mesh axis runs over, the one named last changes fastest.
Arguments:
- a_tiles: float32 [4096, 4, 128, 128], P(('gx', 'gy')), may hold values from -6 to 6
- a_cols: int32 [4096, 4], P(('gx', 'gy')), may hold values from 0 to 4095, as said below
- new_row: int32 [4096], P(('gx', 'gy')), may hold values from 0 to 4095, as said below
- p_tiles: float32 [4096, 2, 128, 128], P(('gx', 'gy')), may hold values from -0.5 to 0.5
- p_cols: int32 [4096, 2], P(('gx', 'gy')), may hold values from 0 to 1023, as said below
Outputs:
- coarse: float32 [1024, 10, 128, 128], P(('gx', 'gy'))
The draws below stay inside these ranges and needn't reach their ends.
Inputs may be any that keep to these rules, and one draw needn't show every extreme that they name: A permutation; the new owner new_row // 8 of a block row has the same gy index as its old owner and a gx index 0 to 5 above the old owner's, modulo the number of gx indices; at most 2 block rows of one device go to one new owner. `a_cols`: the first column block of old block row o is new_row[o]; the others are distinct block rows of the devices with the same gx index as new_row[o]'s owner and gy index one below, equal or one above. `p_cols`: for block row g owned by device d (gy index y), the first coarse block is one of d's 2 coarse blocks, the second one of device d + 1's, or of d's where y is the last gy index.
All inputs are finite; a program needn't handle non-finite values.
Results may differ from the reference program's by a relative error of at most 0.0003.
Values sent between devices are 32-bit elements; how exact they have to be, the bound alone decides.
No kernel may reach another device: no remote copies, remote signals or barrier semaphores. Data moves between devices by JAX's collectives and lax.ppermute only.
A program may use at most 128 MiB of HBM per device.

```python
import jax
import jax.numpy as jnp
from jax import lax

TILE = 128
ROWS_DEV = 8
GROUPS = 4
A_TILES = 4
P_TILES = 2
SPAN = 6
CAP = 2
COARSE_DEV = 2
SLOTS = 10
NB = 4096
NC = 1024
N_GX = 16
N_GY = 32


def migration(key):
    first_key, second_key = jax.random.split(jax.random.fold_in(key, 11))
    scores = jax.random.randint(first_key, (N_GY, SPAN), 0, 1 << 20) * 64 + jnp.arange(SPAN)[None, :]
    offsets = jnp.argsort(scores, axis=1)[:, :GROUPS]
    slot_scores = jax.random.randint(second_key, (N_GX, N_GY, ROWS_DEV), 0, 1 << 20) * 256 + jnp.arange(ROWS_DEV)[None, None, :]
    position = jnp.argsort(slot_scores, axis=2).astype(jnp.int32)
    group_id = position // CAP
    within = position % CAP
    column_y = jnp.broadcast_to(jnp.arange(N_GY)[None, :, None], position.shape)
    source_x = jnp.broadcast_to(jnp.arange(N_GX)[:, None, None], position.shape)
    target_x = (source_x + offsets[column_y, group_id]) % N_GX
    result = (target_x * N_GY + column_y) * ROWS_DEV + group_id * CAP + within
    return result.reshape(-1).astype(jnp.int32)


def draw_new_row(key, part):
    return migration(key)


def draw_a_cols(key, part):
    moved_to = migration(key)
    pick_key = jax.random.fold_in(key, 23)
    total = ROWS_DEV * N_GX * N_GY
    block_row = jnp.arange(total)
    device_id = block_row // ROWS_DEV
    column_y = device_id % N_GY
    window = jnp.arange(3 * ROWS_DEV)
    cand_y = column_y[:, None] - 1 + window[None, :] // ROWS_DEV
    candidate = (device_id[:, None] - 1 + window[None, :] // ROWS_DEV) * ROWS_DEV + window[None, :] % ROWS_DEV
    usable = (cand_y >= 0) & (cand_y < N_GY) & (candidate != block_row[:, None])
    scores = jax.random.randint(pick_key, (total, 3 * ROWS_DEV), 0, 1 << 20) * 512 + window[None, :]
    scores = jnp.where(usable, scores, 1 << 30)
    order_index = jnp.argsort(scores, axis=1)[:, :A_TILES - 1]
    chosen = jnp.take_along_axis(candidate, order_index, axis=1)
    columns_new = jnp.concatenate([block_row[:, None], chosen], axis=1).astype(jnp.int32)
    return columns_new[moved_to]


def draw_p_cols(key, part):
    first_key, second_key = jax.random.split(jax.random.fold_in(key, 37))
    total = ROWS_DEV * N_GX * N_GY
    device_id = jnp.arange(total) // ROWS_DEV
    column_y = device_id % N_GY
    first_block = jax.random.randint(first_key, (total,), 0, COARSE_DEV)
    second_block = jax.random.randint(second_key, (total,), 0, COARSE_DEV)
    next_device = jnp.where(column_y < N_GY - 1, device_id + 1, device_id)
    return jnp.stack([device_id * COARSE_DEV + first_block, next_device * COARSE_DEV + second_block], axis=1).astype(jnp.int32)


def levels(own_key, dims, pieces, low, largest):
    factor_of = 1.0
    for dim, parts in pieces:
        steps = jax.random.uniform(jax.random.fold_in(jax.random.fold_in(own_key, 6), dim), (parts,), jnp.float32, low / len(pieces), largest / len(pieces))
        factor_of = factor_of * jnp.repeat(jnp.exp(steps), dims[dim] // parts).reshape((-1,) + (1,) * (len(dims) - 1 - dim))
    return factor_of


def normal_values(own_key, shape, width, limit, shards=(), dtype=jnp.bfloat16):
    level = levels(own_key, shape, shards, -0.22, 0.18) if shards else 1.0
    array = jax.random.normal(own_key, shape, jnp.float32) * width * level
    return jnp.minimum(jnp.maximum(array, -limit), limit).astype(dtype)


def setup_inputs(seed: int = 0) -> dict:
    splits = jax.random.split(jax.random.key(seed), 6)
    a_tiles = normal_values(splits[0], (NB, A_TILES, TILE, TILE), 1.0, 6.0, ((0, 512),), jnp.float32)
    a_cols = draw_a_cols(jax.random.fold_in(splits[5], 71), 0)
    new_row = draw_new_row(jax.random.fold_in(splits[5], 71), 0)
    p_tiles = normal_values(splits[3], (NB, P_TILES, TILE, TILE), TILE ** -0.5, 0.5, ((0, 512),), jnp.float32)
    p_cols = draw_p_cols(jax.random.fold_in(splits[5], 71), 0)
    return {"a_tiles": a_tiles, "a_cols": a_cols, "new_row": new_row, "p_tiles": p_tiles, "p_cols": p_cols}


def reference(a_tiles, a_cols, new_row, p_tiles, p_cols):
    moved = jnp.zeros_like(a_tiles).at[new_row].set(a_tiles)
    moved_cols = jnp.zeros_like(a_cols).at[new_row].set(a_cols)
    coarse = jnp.zeros((NC, SLOTS, TILE, TILE), jnp.float32)

    def add_row(total, row_data):
        tiles, columns, own_tiles, own_cols = row_data
        fetched = p_tiles[columns]
        products = jnp.einsum("kab,kqbc->kqac", tiles, fetched, precision=lax.Precision.HIGHEST)
        targets = p_cols[columns]
        terms = jnp.einsum("pba,kqbc->pkqac", own_tiles, products, precision=lax.Precision.HIGHEST)
        relative = targets[None, :, :] // COARSE_DEV - own_cols[:, None, None] // COARSE_DEV + 2
        slot_index = relative * COARSE_DEV + targets[None, :, :] % COARSE_DEV
        row_index = jnp.broadcast_to(own_cols[:, None, None], slot_index.shape)
        total = total.at[row_index.reshape(-1), slot_index.reshape(-1)].add(terms.reshape(-1, TILE, TILE))
        return total, None

    coarse, unused = lax.scan(add_row, coarse, (moved, moved_cols, p_tiles, p_cols))
    return coarse
```

```python
import functools

import jax
import jax.numpy as jnp
from jax import lax
from jax.experimental import pallas as pl
from jax.experimental.pallas import tpu as pltpu
from jax.sharding import PartitionSpec as P

TILE = 128
A_TILES = 4
P_TILES = 2
CAP = 2
SPAN = 6
SLOTS = 10
ROW = A_TILES * TILE
META = 8
WIDTHS = (SLOTS, SLOTS - 2)

BUFFERS = {
    "far": (((10, 0, ROW), (11, 0, ROW - TILE)), True),
    "up": (((11, ROW - TILE, TILE),), False),
    "d4": (((8, 0, ROW), (9, 0, ROW)), True),
    "d3": (((6, 0, ROW), (7, 0, ROW)), True),
    "d2": (((4, 0, ROW), (5, 0, ROW)), True),
    "d1": (((2, 0, ROW), (3, 0, ROW)), True),
    "d0": (((0, 0, ROW), (1, 0, ROW)), True),
}

ANY = pl.BlockSpec(memory_space=pl.ANY)
SMEM = pl.BlockSpec(memory_space=pltpu.SMEM)
VMEM = pl.BlockSpec(memory_space=pltpu.VMEM)


def hop(value, axis, steps):
    count = lax.axis_size(axis)
    return lax.ppermute(value, axis, [(i, (i + steps) % count) for i in range(count)])


def beside(value, steps):
    count = lax.axis_size("gy")
    route = [(i, i + steps) for i in range(count) if 0 <= i + steps < count]
    return lax.ppermute(value, "gy", route)


def bucket_kernel(rows, gx, per_x, layout, new_row, a_cols, my_x, a_hbm, *refs):
    outs = refs[: len(BUFFERS)]
    held, notes, order, in_sem, out_sem, note_sem = refs[len(BUFFERS) :]
    loads = [pltpu.make_async_copy(a_hbm.at[o], held.at[o], in_sem.at[o]) for o in range(rows)]
    for load in loads:
        load.start()
    for s in range(SPAN * CAP):
        order[s] = -1
    gaps = [lax.rem(lax.div(new_row[o], per_x) - my_x[0] + gx, gx) for o in range(rows)]
    for o in range(rows):
        rank = sum([(gaps[e] == gaps[o]).astype(jnp.int32) for e in range(o)], jnp.int32(0))
        order[gaps[o] * CAP + rank] = o
    lane = lax.broadcasted_iota(jnp.int32, (META, TILE), 1)
    line = lax.broadcasted_iota(jnp.int32, (META, TILE), 0)
    note_copies = []
    for b, (pieces, noted) in enumerate(layout):
        if not noted:
            continue
        note = jnp.zeros((META, TILE), jnp.int32)
        for r, (s, _, _) in enumerate(pieces[:CAP]):
            o = order[s]
            here = jnp.maximum(o, 0)
            place = jnp.where(o >= 0, lax.rem(new_row[here], rows) + 1, 0)
            for k in range(A_TILES):
                note = jnp.where((line == r) & (lane == k), a_cols[here * A_TILES + k], note)
            note = jnp.where((line == r) & (lane == A_TILES), place, note)
        notes[b] = note.astype(jnp.float32)
        size = sum(n for _, _, n in pieces)
        copy = pltpu.make_async_copy(notes.at[b], outs[b].at[pl.ds(size, META)], note_sem.at[b])
        copy.start()
        note_copies.append(copy)
    for load in loads:
        load.wait()

    def each(act):
        n = 0
        for out, (pieces, _) in zip(outs, layout):
            to = 0
            for s, frm, size in pieces:
                o = order[s]
                here = jnp.maximum(o, 0)

                @pl.when(o >= 0)
                def _():
                    act(
                        pltpu.make_async_copy(
                            held.at[here, pl.ds(frm, size)], out.at[pl.ds(to, size)], out_sem.at[n]
                        )
                    )

                to += size
                n += 1

    each(lambda copy: copy.start())
    each(lambda copy: copy.wait())
    for copy in note_copies:
        copy.wait()


def buckets(a_tiles, a_cols, new_row, my_x):
    rows = a_tiles.shape[0]
    gx, gy = lax.axis_size("gx"), lax.axis_size("gy")
    layout = list(BUFFERS.values())
    lengths = [sum(n for _, _, n in pieces) + META * noted for pieces, noted in layout]
    outs = pl.pallas_call(
        functools.partial(bucket_kernel, rows, gx, rows * gy, layout),
        out_shape=[jax.ShapeDtypeStruct((n, TILE), jnp.float32) for n in lengths],
        in_specs=[SMEM, SMEM, SMEM, ANY],
        out_specs=[ANY] * len(lengths),
        scratch_shapes=[
            pltpu.VMEM((rows, ROW, TILE), jnp.float32),
            pltpu.VMEM((len(lengths), META, TILE), jnp.float32),
            pltpu.SMEM((SPAN * CAP,), jnp.int32),
            pltpu.SemaphoreType.DMA((rows,)),
            pltpu.SemaphoreType.DMA((sum(len(p) for p, _ in layout),)),
            pltpu.SemaphoreType.DMA((len(lengths),)),
        ],
        compiler_params=pltpu.CompilerParams(vmem_limit_bytes=4 * 2**20),
        name="buckets",
    )(new_row, a_cols.reshape(-1), my_x, a_tiles.reshape(rows, ROW, TILE))
    return dict(zip(BUFFERS, outs))


def halves(x):
    high = x.astype(jnp.bfloat16)
    return high, (x - high.astype(jnp.float32)).astype(jnp.bfloat16)


def split_kernel(rows, *refs):
    sources, (high, low, turned) = refs[:3], refs[3:]
    for n, source in enumerate(sources):

        def body(i, carry):
            for q in range(P_TILES):
                block = source[pl.ds(pl.multiple_of((i * P_TILES + q) * TILE, TILE), TILE), :]
                h, l = halves(block)
                high[n * rows + i, :, q * TILE : (q + 1) * TILE] = h
                low[n * rows + i, :, q * TILE : (q + 1) * TILE] = l
                if n == 1:
                    h, l = halves(block.T)
                    turned[i * P_TILES + q, :TILE, :] = h
                    turned[i * P_TILES + q, TILE:, :] = l
            return carry

        lax.fori_loop(0, rows, body, 0)


def split(sources, rows):
    wide = jax.ShapeDtypeStruct((3 * rows, TILE, P_TILES * TILE), jnp.bfloat16)
    return pl.pallas_call(
        functools.partial(split_kernel, rows),
        out_shape=[wide, wide, jax.ShapeDtypeStruct((rows * P_TILES, 2 * TILE, TILE), jnp.bfloat16)],
        in_specs=[VMEM] * 3,
        out_specs=[VMEM] * 3,
        name="split",
    )(*sources)


def galerkin_kernel(rows, chunks, targets, fresh, slots, first, high, low, turned, *refs):
    count = sum(len(c) for c in chunks)
    buffers, refs = refs[:count], refs[count:]
    if not fresh:
        befores, refs = refs[: len(targets)], refs[len(targets) :]
    accs, refs = refs[: len(targets)], refs[len(targets) :]
    lifted, held, notes, note_sem, sem = refs
    at, note_copies, lines = 0, [], []
    for n, lengths in enumerate(chunks):
        parts = buffers[at : at + len(lengths)]
        at += len(lengths)
        end = lengths[0][0] - META
        copy = pltpu.make_async_copy(parts[0].at[pl.ds(end, META)], notes.at[n], note_sem.at[n])
        copy.start()
        note_copies.append(copy)
        for r in range(CAP):
            size = min(ROW, end - r * ROW)
            pieces = [(parts[0], r * ROW, 0, size)]
            if size < ROW:
                pieces.append((parts[1], lengths[1][1], size, ROW - size))
            lines.append((n, r, pieces))
    for i, acc in enumerate(accs):
        if fresh:
            acc[...] = jnp.zeros_like(acc)
        else:
            acc[...] = befores[i][...]
    for copy in note_copies:
        copy.wait()

    def note(n, r, k):
        return notes[n, r, k].astype(jnp.int32)

    def copies(m):
        return [
            pltpu.make_async_copy(
                part.at[pl.ds(frm, size)], held.at[m, pl.ds(to, size)], sem.at[2 * m + i]
            )
            for i, (part, frm, to, size) in enumerate(lines[m][2])
        ]

    for m, (n, r, _) in enumerate(lines):

        @pl.when(note(n, r, A_TILES) > 0)
        def _():
            for copy in copies(m):
                copy.start()

    for m, (n, r, _) in enumerate(lines):

        @pl.when(note(n, r, A_TILES) > 0)
        def _():
            for copy in copies(m):
                copy.wait()
            row = note(n, r, A_TILES) - 1
            cols = [note(n, r, k) - first[0] for k in range(A_TILES)]
            for k, c in enumerate(cols):
                h, l = halves(held[m, k * TILE : (k + 1) * TILE, :])
                left = jnp.concatenate([h, l], axis=1)
                t = jnp.dot(
                    left, jnp.concatenate([high[c], high[c]], axis=0), preferred_element_type=jnp.float32
                ) + jnp.dot(
                    left, jnp.concatenate([low[c], low[c]], axis=0), preferred_element_type=jnp.float32
                )
                h, l = halves(t)
                span = slice(k * P_TILES * TILE, (k + 1) * P_TILES * TILE)
                lifted[:TILE, span] = h
                lifted[TILE:, span] = l
            for p in range(P_TILES):
                for target, acc in zip(targets, accs):
                    mine = slots[rows + row, p] - 4 - 2 * target

                    @pl.when((mine == 0) | (mine == 1))
                    def _():
                        left = turned[row * P_TILES + p]
                        w = jnp.dot(
                            jnp.concatenate([left, left], axis=1), lifted[...], preferred_element_type=jnp.float32
                        )
                        w = w[:TILE] + w[TILE:]
                        for k, c in enumerate(cols):
                            for q in range(P_TILES):
                                lanes = (k * P_TILES + q) * TILE
                                s = mine * WIDTHS[target] + slots[c, q] - 2 * target
                                acc[s] += w[:, lanes : lanes + TILE]


def galerkin(weight, chunks, targets, first_row, slots, splits, befores, rows, coarse_rows):
    shapes = [tuple((x.shape[0], frm) for x, frm in parts) for parts in chunks]
    buffers = [x for parts in chunks for x, _ in parts]
    out = [jax.ShapeDtypeStruct((coarse_rows * WIDTHS[t], TILE, TILE), jnp.float32) for t in targets]
    befores = befores or []
    operands = [slots, first_row, *splits, *buffers, *befores]
    specs = [SMEM, SMEM] + [VMEM] * len(splits) + [ANY] * len(buffers) + [VMEM] * len(befores)
    lines = CAP * len(chunks)
    return pl.pallas_call(
        functools.partial(galerkin_kernel, rows, shapes, targets, not befores),
        out_shape=out,
        in_specs=specs,
        out_specs=[VMEM] * len(out),
        scratch_shapes=[
            pltpu.VMEM((2 * TILE, A_TILES * P_TILES * TILE), jnp.bfloat16),
            pltpu.VMEM((lines, ROW, TILE), jnp.float32),
            pltpu.SMEM((len(chunks), META, TILE), jnp.float32),
            pltpu.SemaphoreType.DMA((len(chunks),)),
            pltpu.SemaphoreType.DMA((2 * lines,)),
        ],
        input_output_aliases={len(operands) - len(befores) + i: i for i in range(len(befores))},
        compiler_params=pltpu.CompilerParams(vmem_limit_bytes=20 * 2**20),
        cost_estimate=pl.CostEstimate(flops=weight, bytes_accessed=1, transcendentals=0),
        name="galerkin",
    )(*operands)


def after(value, *others):
    return lax.optimization_barrier((value, *others))[0]


def shards(a_tiles, a_cols, new_row, p_tiles, p_cols):
    rows = a_tiles.shape[0]
    coarse_rows = rows // 4
    my_x = lax.axis_index("gx").astype(jnp.int32)
    device = my_x * lax.axis_size("gy") + lax.axis_index("gy").astype(jnp.int32)

    p_notes = jnp.pad(p_cols.astype(jnp.float32), ((0, 0), (0, TILE - P_TILES)))
    p_here = jnp.concatenate([p_tiles.reshape(-1, TILE), p_notes], axis=0)
    sources = [beside(p_here, 1), p_here, beside(p_here, -1)]

    send = buckets(a_tiles, a_cols, new_row, my_x.reshape(1))
    d1 = hop(after(send["d1"], sources[2], sources[0]), "gx", 1)
    d2 = hop(after(send["d2"], sources[0]), "gx", 2)
    d3 = hop(send["d3"], "gx", 3)
    d4 = hop(send["d4"], "gx", 4)
    far = hop(send["far"], "gx", -6)

    slots = jnp.concatenate([x[-rows:, :P_TILES] for x in sources], axis=0).astype(jnp.int32)
    slots = slots - coarse_rows * device + 4
    splits = split(sources, rows)
    first_row = ((device - 1) * rows).reshape(1)

    def add(targets, chunks, befores, weight=1):
        return galerkin(weight, chunks, targets, first_row, slots, splits, befores, rows, coarse_rows)

    both = add((0, 1), [[(send["d0"], 0)]], None, 10**14)
    up = hop(after(send["up"], far, both[0]), "gx", 5)
    far = hop(after(far, both[0]), "gx", -5)
    both = add((0, 1), [[(d4, 0)]], both)
    both = add((0, 1), [[(d3, 0)]], both)
    own, on = add((0, 1), [[(d2, 0)]], both)
    last = [[(d1, 0)], [(far, 0), (up, 0)]]
    (on,) = add((1,), last, [on])
    arrived = beside(on, 1)
    (own,) = add((0,), last, [own])
    own = own.reshape(coarse_rows, SLOTS, TILE, TILE)
    arrived = arrived.reshape(coarse_rows, WIDTHS[1], TILE, TILE)
    return own + jnp.pad(arrived, ((0, 0), (0, SLOTS - WIDTHS[1]), (0, 0), (0, 0)))


def solution(mesh):
    in_specs = (
        P(("gx", "gy"), None, None, None),
        P(("gx", "gy"), None),
        P(("gx", "gy")),
        P(("gx", "gy"), None, None, None),
        P(("gx", "gy"), None),
    )
    out_specs = P(("gx", "gy"), None, None, None)
    return jax.shard_map(shards, mesh=mesh, in_specs=in_specs, out_specs=out_specs, check_vma=False)
```

```python
import functools

import jax
import jax.numpy as jnp
from jax import lax
from jax.experimental import pallas as pl
from jax.experimental.pallas import tpu as pltpu
from jax.sharding import PartitionSpec as P

TILE = 128
A_TILES = 4
P_TILES = 2
CAP = 2
SPAN = 6
SLOTS = 10
ROW = A_TILES * TILE
META = 8
WIDTHS = (SLOTS, SLOTS - 2)

BUFFERS = {
    "far_a": (((10, 0, ROW),), True),
    "far_b": (((11, 0, ROW - TILE),), True),
    "d4": (((8, 0, ROW), (9, 0, ROW), (11, ROW - TILE, TILE)), True),
    "d3": (((6, 0, ROW), (7, 0, ROW)), True),
    "d2": (((4, 0, ROW), (5, 0, ROW)), True),
    "d1": (((2, 0, ROW), (3, 0, ROW), (None, 0, TILE)), True),
    "d0": (((0, 0, ROW), (1, 0, ROW)), True),
}

ANY = pl.BlockSpec(memory_space=pl.ANY)
HBM = pl.BlockSpec(memory_space=pltpu.MemorySpace.HBM)
SMEM = pl.BlockSpec(memory_space=pltpu.SMEM)
VMEM = pl.BlockSpec(memory_space=pltpu.VMEM)


def hop(value, axis, steps):
    count = lax.axis_size(axis)
    return lax.ppermute(value, axis, [(i, (i + steps) % count) for i in range(count)])


def beside(value, steps):
    count = lax.axis_size("gy")
    route = [(i, i + steps) for i in range(count) if 0 <= i + steps < count]
    return lax.ppermute(value, "gy", route)


def bucket_kernel(rows, gx, per_x, layout, new_row, a_cols, p_cols, my_x, a_hbm, p_hbm, *refs):
    p_out, outs = refs[0], refs[1 : 1 + len(BUFFERS)]
    held, held_p, notes, order, in_sem, out_sem, note_sem, p_sem = refs[1 + len(BUFFERS) :]
    p_size = rows * P_TILES * TILE
    p_load = pltpu.make_async_copy(p_hbm, held_p.at[pl.ds(0, p_size)], p_sem)
    p_load.start()
    loads = [pltpu.make_async_copy(a_hbm.at[o], held.at[o], in_sem.at[o]) for o in range(rows)]
    for load in loads:
        load.start()
    for s in range(SPAN * CAP):
        order[s] = -1
    gaps = [lax.rem(lax.div(new_row[o], per_x) - my_x[0] + gx, gx) for o in range(rows)]
    for o in range(rows):
        rank = sum([(gaps[e] == gaps[o]).astype(jnp.int32) for e in range(o)], jnp.int32(0))
        order[gaps[o] * CAP + rank] = o
    lane = lax.broadcasted_iota(jnp.int32, (META, TILE), 1)
    line = lax.broadcasted_iota(jnp.int32, (META, TILE), 0)
    note_copies = []
    for b, (pieces, noted) in enumerate(layout):
        if not noted:
            continue
        note = jnp.zeros((META, TILE), jnp.int32)
        for r, (s, _, _) in enumerate(pieces[:CAP]):
            o = order[s]
            here = jnp.maximum(o, 0)
            place = jnp.where(o >= 0, lax.rem(new_row[here], rows) + 1, 0)
            for k in range(A_TILES):
                note = jnp.where((line == r) & (lane == k), a_cols[here, k], note)
            note = jnp.where((line == r) & (lane == A_TILES), place, note)
        notes[b] = note.astype(jnp.float32)
        size = sum(n for _, _, n in pieces)
        copy = pltpu.make_async_copy(notes.at[b], outs[b].at[pl.ds(size, META)], note_sem.at[b])
        copy.start()
        note_copies.append(copy)
    note = jnp.zeros((META, TILE), jnp.int32)
    for i in range(rows):
        for q in range(P_TILES):
            note = jnp.where((line == i) & (lane == q), p_cols[i, q], note)
    held_p[p_size:, :] = note.astype(jnp.float32)
    p_load.wait()
    p_copy = pltpu.make_async_copy(held_p, p_out, p_sem)
    p_copy.start()
    for load in loads:
        load.wait()

    def each(act):
        n = 0
        for out, (pieces, _) in zip(outs, layout):
            to = 0
            for s, frm, size in pieces:
                if s is None:
                    continue
                o = order[s]
                here = jnp.maximum(o, 0)

                @pl.when(o >= 0)
                def _():
                    act(
                        pltpu.make_async_copy(
                            held.at[here, pl.ds(frm, size)], out.at[pl.ds(to, size)], out_sem.at[n]
                        )
                    )

                to += size
                n += 1

    each(lambda copy: copy.start())
    each(lambda copy: copy.wait())
    for copy in note_copies:
        copy.wait()
    p_copy.wait()


def buckets(a_tiles, a_cols, new_row, p_tiles, p_cols, my_x):
    rows = a_tiles.shape[0]
    gx, gy = lax.axis_size("gx"), lax.axis_size("gy")
    layout = list(BUFFERS.values())
    lengths = [sum(n for _, _, n in pieces) + META * noted for pieces, noted in layout]
    p_lines = rows * P_TILES * TILE
    p_here, *outs = pl.pallas_call(
        functools.partial(bucket_kernel, rows, gx, rows * gy, layout),
        out_shape=[jax.ShapeDtypeStruct((n, TILE), jnp.float32) for n in [p_lines + META] + lengths],
        in_specs=[SMEM, SMEM, SMEM, SMEM, HBM, HBM],
        out_specs=[HBM] * (1 + len(lengths)),
        scratch_shapes=[
            pltpu.VMEM((rows, ROW, TILE), jnp.float32),
            pltpu.VMEM((p_lines + META, TILE), jnp.float32),
            pltpu.VMEM((len(lengths), META, TILE), jnp.float32),
            pltpu.SMEM((SPAN * CAP,), jnp.int32),
            pltpu.SemaphoreType.DMA((rows,)),
            pltpu.SemaphoreType.DMA((sum(len(p) for p, _ in layout),)),
            pltpu.SemaphoreType.DMA((len(lengths),)),
            pltpu.SemaphoreType.DMA,
        ],
        compiler_params=pltpu.CompilerParams(vmem_limit_bytes=5 * 2**20),
        name="buckets",
    )(new_row, a_cols, p_cols, my_x, a_tiles.reshape(rows, ROW, TILE), p_tiles.reshape(p_lines, TILE))
    return p_here, dict(zip(BUFFERS, outs))


def halves(x):
    high = x.astype(jnp.bfloat16)
    return high, (x - high.astype(jnp.float32)).astype(jnp.bfloat16)


def split_kernel(rows, *refs):
    sources, (high, low, turned) = refs[:3], refs[3:]
    for n, source in enumerate(sources):

        def body(i, carry):
            for q in range(P_TILES):
                block = source[pl.ds(pl.multiple_of((i * P_TILES + q) * TILE, TILE), TILE), :]
                h, l = halves(block)
                high[n * rows + i, :, q * TILE : (q + 1) * TILE] = h
                low[n * rows + i, :, q * TILE : (q + 1) * TILE] = l
                if n == 1:
                    h, l = halves(block.T)
                    turned[i * P_TILES + q, :TILE, :] = h
                    turned[i * P_TILES + q, TILE:, :] = l
            return carry

        lax.fori_loop(0, rows, body, 0)


def split(sources, rows):
    wide = jax.ShapeDtypeStruct((3 * rows, TILE, P_TILES * TILE), jnp.bfloat16)
    return pl.pallas_call(
        functools.partial(split_kernel, rows),
        out_shape=[wide, wide, jax.ShapeDtypeStruct((rows * P_TILES, 2 * TILE, TILE), jnp.bfloat16)],
        in_specs=[VMEM] * 3,
        out_specs=[VMEM] * 3,
        compiler_params=pltpu.CompilerParams(vmem_limit_bytes=12 * 2**20),
        name="split",
    )(*sources)


def galerkin_kernel(rows, chunks, targets, fresh, slots, first, high, low, turned, *refs):
    count = sum(len(c) for c in chunks)
    buffers, refs = refs[:count], refs[count:]
    if not fresh:
        befores, refs = refs[: len(targets)], refs[len(targets) :]
    accs, refs = refs[: len(targets)], refs[len(targets) :]
    lifted, held, notes, note_sem, sem = refs
    at, note_copies, lines = 0, [], []
    for n, lengths in enumerate(chunks):
        parts = buffers[at : at + len(lengths)]
        at += len(lengths)
        end = lengths[0][0] - META
        copy = pltpu.make_async_copy(parts[0].at[pl.ds(end, META)], notes.at[n], note_sem.at[n])
        copy.start()
        note_copies.append(copy)
        for r in range(min(CAP, -(-end // ROW))):
            size = min(ROW, end - r * ROW)
            pieces = [(parts[0], r * ROW, 0, size)]
            if size < ROW:
                pieces.append((parts[1], lengths[1][1], size, ROW - size))
            lines.append((n, r, pieces))
    for i, acc in enumerate(accs):
        if fresh:
            acc[...] = jnp.zeros_like(acc)
        else:
            acc[...] = befores[i][...]
    for copy in note_copies:
        copy.wait()

    def note(n, r, k):
        return notes[n, r, k].astype(jnp.int32)

    def copies(m):
        return [
            pltpu.make_async_copy(
                part.at[pl.ds(frm, size)], held.at[m, pl.ds(to, size)], sem.at[2 * m + i]
            )
            for i, (part, frm, to, size) in enumerate(lines[m][2])
        ]

    for m, (n, r, _) in enumerate(lines):

        @pl.when(note(n, r, A_TILES) > 0)
        def _():
            for copy in copies(m):
                copy.start()

    for m, (n, r, _) in enumerate(lines):

        @pl.when(note(n, r, A_TILES) > 0)
        def _():
            for copy in copies(m):
                copy.wait()
            row = note(n, r, A_TILES) - 1
            cols = [note(n, r, k) - first[0] for k in range(A_TILES)]
            for k, c in enumerate(cols):
                h, l = halves(held[m, k * TILE : (k + 1) * TILE, :])
                left = jnp.concatenate([h, l], axis=1)
                t = jnp.dot(
                    left, jnp.concatenate([high[c], high[c]], axis=0), preferred_element_type=jnp.float32
                ) + jnp.dot(
                    left, jnp.concatenate([low[c], low[c]], axis=0), preferred_element_type=jnp.float32
                )
                h, l = halves(t)
                span = slice(k * P_TILES * TILE, (k + 1) * P_TILES * TILE)
                lifted[:TILE, span] = h
                lifted[TILE:, span] = l
            for p in range(P_TILES):
                for target, acc in zip(targets, accs):
                    mine = slots[rows + row, p] - 4 - 2 * target

                    @pl.when((mine == 0) | (mine == 1))
                    def _():
                        left = turned[row * P_TILES + p]
                        w = jnp.dot(
                            jnp.concatenate([left, left], axis=1), lifted[...], preferred_element_type=jnp.float32
                        )
                        w = w[:TILE] + w[TILE:]
                        for k, c in enumerate(cols):
                            for q in range(P_TILES):
                                lanes = (k * P_TILES + q) * TILE
                                s = mine * WIDTHS[target] + slots[c, q] - 2 * target
                                acc[s] += w[:, lanes : lanes + TILE]


def galerkin(weight, chunks, targets, first_row, slots, splits, befores, rows, coarse_rows):
    shapes = [tuple((x.shape[0], frm) for x, frm in parts) for parts in chunks]
    buffers = [x for parts in chunks for x, _ in parts]
    out = [jax.ShapeDtypeStruct((coarse_rows * WIDTHS[t], TILE, TILE), jnp.float32) for t in targets]
    befores = befores or []
    operands = [slots, first_row, *splits, *buffers, *befores]
    specs = [SMEM, SMEM] + [VMEM] * len(splits) + [ANY] * len(buffers) + [VMEM] * len(befores)
    lines = sum(min(CAP, -(-(parts[0][0] - META) // ROW)) for parts in shapes)
    return pl.pallas_call(
        functools.partial(galerkin_kernel, rows, shapes, targets, not befores),
        out_shape=out,
        in_specs=specs,
        out_specs=[VMEM] * len(out),
        scratch_shapes=[
            pltpu.VMEM((2 * TILE, A_TILES * P_TILES * TILE), jnp.bfloat16),
            pltpu.VMEM((lines, ROW, TILE), jnp.float32),
            pltpu.SMEM((len(chunks), META, TILE), jnp.float32),
            pltpu.SemaphoreType.DMA((len(chunks),)),
            pltpu.SemaphoreType.DMA((2 * lines,)),
        ],
        input_output_aliases={len(operands) - len(befores) + i: i for i in range(len(befores))},
        compiler_params=pltpu.CompilerParams(vmem_limit_bytes=20 * 2**20),
        cost_estimate=pl.CostEstimate(flops=weight, bytes_accessed=1, transcendentals=0),
        name="galerkin",
    )(*operands)


def after(value, *others):
    return lax.optimization_barrier((value, *others))[0]


def shards(a_tiles, a_cols, new_row, p_tiles, p_cols):
    rows = a_tiles.shape[0]
    coarse_rows = rows // 4
    my_x = lax.axis_index("gx").astype(jnp.int32)
    device = my_x * lax.axis_size("gy") + lax.axis_index("gy").astype(jnp.int32)

    p_here, send = buckets(a_tiles, a_cols, new_row, p_tiles, p_cols, my_x.reshape(1))
    p_before = beside(p_here, 1)
    p_after = beside(p_here, -1)
    sources = [p_before, p_here, p_after]
    d4 = hop(send["d4"], "gx", 4)
    far_a = hop(send["far_a"], "gx", -6)
    d3 = hop(after(send["d3"], p_after), "gx", 3)
    far_b = hop(after(send["far_b"], p_after), "gx", -6)
    d2 = hop(after(send["d2"], p_before, p_after), "gx", 2)

    slots = jnp.concatenate([x[-rows:, :P_TILES] for x in sources], axis=0).astype(jnp.int32)
    slots = slots - coarse_rows * device + 4
    splits = split(sources, rows)
    first_row = ((device - 1) * rows).reshape(1)

    def add(targets, chunks, befores, weight=1):
        return galerkin(weight, chunks, targets, first_row, slots, splits, befores, rows, coarse_rows)

    both = add((0, 1), [[(send["d0"], 0)]], None, 10**14)
    far_a = hop(after(far_a, p_before, p_after), "gx", -5)
    far_b = hop(after(far_b, both[0]), "gx", -5)
    end = CAP * ROW
    d4 = after(d4, both[0])
    d1 = hop(lax.dynamic_update_slice(send["d1"], d4[end : end + TILE], (end, 0)), "gx", 1)
    both = add((0, 1), [[(d4, 0)]], both, 10**14)
    both = add((0, 1), [[(d3, 0)]], both)
    own, on = add((0, 1), [[(d2, 0)], [(far_a, 0)]], both)
    last = [[(d1, 0)], [(far_b, 0), (d1, end)]]
    (on,) = add((1,), last, [on])
    arrived = beside(on, 1)
    (own,) = add((0,), last, [own])
    own = own.reshape(coarse_rows, SLOTS, TILE, TILE)
    arrived = arrived.reshape(coarse_rows, WIDTHS[1], TILE, TILE)
    return own + jnp.pad(arrived, ((0, 0), (0, SLOTS - WIDTHS[1]), (0, 0), (0, 0)))


def solution(mesh):
    in_specs = (
        P(("gx", "gy"), None, None, None),
        P(("gx", "gy"), None),
        P(("gx", "gy")),
        P(("gx", "gy"), None, None, None),
        P(("gx", "gy"), None),
    )
    out_specs = P(("gx", "gy"), None, None, None)
    return jax.shard_map(shards, mesh=mesh, in_specs=in_specs, out_specs=out_specs, check_vma=False)
```

```python
import functools

import jax
import jax.numpy as jnp
from jax import lax
from jax.experimental import pallas as pl
from jax.experimental.pallas import tpu as pltpu
from jax.sharding import PartitionSpec as P

TILE = 128
A_TILES = 4
P_TILES = 2
CAP = 2
SPAN = 6
SLOTS = 10
ROW = A_TILES * TILE
META = 8
WIDTHS = (SLOTS, SLOTS - 2)

BUFFERS = {
    "far_a": (((10, 0, ROW),), True),
    "far_b": (((11, 0, ROW),), True),
    "d4": (((8, 0, ROW), (9, 0, ROW)), True),
    "d3": (((6, 0, ROW), (7, 0, ROW)), True),
    "d2": (((4, 0, ROW), (5, 0, ROW)), True),
    "d1": (((2, 0, ROW), (3, 0, ROW)), True),
    "d0": (((0, 0, ROW), (1, 0, ROW)), True),
}

ANY = pl.BlockSpec(memory_space=pl.ANY)
HBM = pl.BlockSpec(memory_space=pltpu.MemorySpace.HBM)
SMEM = pl.BlockSpec(memory_space=pltpu.SMEM)
VMEM = pl.BlockSpec(memory_space=pltpu.VMEM)


def hop(value, axis, steps):
    count = lax.axis_size(axis)
    return lax.ppermute(value, axis, [(i, (i + steps) % count) for i in range(count)])


def beside(value, steps):
    count = lax.axis_size("gy")
    route = [(i, i + steps) for i in range(count) if 0 <= i + steps < count]
    return lax.ppermute(value, "gy", route)


def bucket_kernel(rows, gx, per_x, layout, new_row, a_cols, p_cols, my_x, a_hbm, p_hbm, *refs):
    p_out, outs = refs[0], refs[1 : 1 + len(BUFFERS)]
    held, held_p, notes, order, in_sem, out_sem, note_sem, p_sem = refs[1 + len(BUFFERS) :]
    p_size = rows * P_TILES * TILE
    p_load = pltpu.make_async_copy(p_hbm, held_p.at[pl.ds(0, p_size)], p_sem)
    p_load.start()
    loads = [pltpu.make_async_copy(a_hbm.at[o], held.at[o], in_sem.at[o]) for o in range(rows)]
    for load in loads:
        load.start()
    for s in range(SPAN * CAP):
        order[s] = -1
    gaps = [lax.rem(lax.div(new_row[o], per_x) - my_x[0] + gx, gx) for o in range(rows)]
    for o in range(rows):
        rank = sum([(gaps[e] == gaps[o]).astype(jnp.int32) for e in range(o)], jnp.int32(0))
        order[gaps[o] * CAP + rank] = o
    lane = lax.broadcasted_iota(jnp.int32, (META, TILE), 1)
    line = lax.broadcasted_iota(jnp.int32, (META, TILE), 0)
    note_copies = []
    for b, (pieces, noted) in enumerate(layout):
        if not noted:
            continue
        note = jnp.zeros((META, TILE), jnp.int32)
        for r, (s, _, _) in enumerate(pieces):
            o = order[s]
            here = jnp.maximum(o, 0)
            place = jnp.where(o >= 0, lax.rem(new_row[here], rows) + 1, 0)
            for k in range(A_TILES):
                note = jnp.where((line == r) & (lane == k), a_cols[k, here], note)
            note = jnp.where((line == r) & (lane == A_TILES), place, note)
        notes[b] = note.astype(jnp.float32)
        size = sum(n for _, _, n in pieces)
        copy = pltpu.make_async_copy(notes.at[b], outs[b].at[pl.ds(size, META)], note_sem.at[b])
        copy.start()
        note_copies.append(copy)
    note = jnp.zeros((META, TILE), jnp.int32)
    for i in range(rows):
        for q in range(P_TILES):
            note = jnp.where((line == i) & (lane == q), p_cols[q, i], note)
    held_p[p_size:, :] = note.astype(jnp.float32)
    p_load.wait()
    p_copy = pltpu.make_async_copy(held_p, p_out, p_sem)
    p_copy.start()
    for load in loads:
        load.wait()

    def each(act):
        n = 0
        for out, (pieces, _) in zip(outs, layout):
            to = 0
            for s, frm, size in pieces:
                o = order[s]
                here = jnp.maximum(o, 0)

                @pl.when(o >= 0)
                def _():
                    act(
                        pltpu.make_async_copy(
                            held.at[here, pl.ds(frm, size)], out.at[pl.ds(to, size)], out_sem.at[n]
                        )
                    )

                to += size
                n += 1

    each(lambda copy: copy.start())
    each(lambda copy: copy.wait())
    for copy in note_copies:
        copy.wait()
    p_copy.wait()


def buckets(a_tiles, a_cols, new_row, p_tiles, p_cols, my_x):
    rows = a_tiles.shape[0]
    gx, gy = lax.axis_size("gx"), lax.axis_size("gy")
    layout = list(BUFFERS.values())
    lengths = [sum(n for _, _, n in pieces) + META * noted for pieces, noted in layout]
    p_lines = rows * P_TILES * TILE
    p_here, *outs = pl.pallas_call(
        functools.partial(bucket_kernel, rows, gx, rows * gy, layout),
        out_shape=[jax.ShapeDtypeStruct((n, TILE), jnp.float32) for n in [p_lines + META] + lengths],
        in_specs=[SMEM, SMEM, SMEM, SMEM, HBM, HBM],
        out_specs=[HBM] * (1 + len(lengths)),
        scratch_shapes=[
            pltpu.VMEM((rows, ROW, TILE), jnp.float32),
            pltpu.VMEM((p_lines + META, TILE), jnp.float32),
            pltpu.VMEM((len(lengths), META, TILE), jnp.float32),
            pltpu.SMEM((SPAN * CAP,), jnp.int32),
            pltpu.SemaphoreType.DMA((rows,)),
            pltpu.SemaphoreType.DMA((sum(len(p) for p, _ in layout),)),
            pltpu.SemaphoreType.DMA((len(lengths),)),
            pltpu.SemaphoreType.DMA,
        ],
        compiler_params=pltpu.CompilerParams(vmem_limit_bytes=60 * 2**20),
        name="buckets",
    )(new_row, a_cols.T, p_cols.T, my_x, a_tiles.reshape(rows, ROW, TILE), p_tiles.reshape(p_lines, TILE))
    return p_here, dict(zip(BUFFERS, outs))


def halves(x):
    high = x.astype(jnp.bfloat16)
    return high, (x - high.astype(jnp.float32)).astype(jnp.bfloat16)


def split_kernel(rows, *refs):
    sources, (high, low, turned) = refs[:3], refs[3:]
    for n, source in enumerate(sources):

        def body(i, carry):
            for q in range(P_TILES):
                block = source[pl.ds(pl.multiple_of((i * P_TILES + q) * TILE, TILE), TILE), :]
                h, l = halves(block)
                high[n * rows + i, :, q * TILE : (q + 1) * TILE] = h
                low[n * rows + i, :, q * TILE : (q + 1) * TILE] = l
                if n == 1:
                    h, l = halves(block.T)
                    turned[i * P_TILES + q, :TILE, :] = h
                    turned[i * P_TILES + q, TILE:, :] = l
            return carry

        lax.fori_loop(0, rows, body, 0)


def split(sources, rows):
    wide = jax.ShapeDtypeStruct((3 * rows, TILE, P_TILES * TILE), jnp.bfloat16)
    return pl.pallas_call(
        functools.partial(split_kernel, rows),
        out_shape=[wide, wide, jax.ShapeDtypeStruct((rows * P_TILES, 2 * TILE, TILE), jnp.bfloat16)],
        in_specs=[VMEM] * 3,
        out_specs=[VMEM] * 3,
        compiler_params=pltpu.CompilerParams(vmem_limit_bytes=12 * 2**20),
        name="split",
    )(*sources)


def galerkin_kernel(rows, chunks, targets, fresh, slots, first, high, low, turned, *refs):
    count = sum(len(c) for c in chunks)
    buffers, refs = refs[:count], refs[count:]
    if not fresh:
        befores, refs = refs[: len(targets)], refs[len(targets) :]
    accs, refs = refs[: len(targets)], refs[len(targets) :]
    lifted, held, notes, note_sem, sem = refs
    at, note_copies, lines = 0, [], []
    for n, lengths in enumerate(chunks):
        parts = buffers[at : at + len(lengths)]
        at += len(lengths)
        end = lengths[0][0] - META
        copy = pltpu.make_async_copy(parts[0].at[pl.ds(end, META)], notes.at[n], note_sem.at[n])
        copy.start()
        note_copies.append(copy)
        for r in range(min(CAP, -(-end // ROW))):
            size = min(ROW, end - r * ROW)
            pieces = [(parts[0], r * ROW, 0, size)]
            if size < ROW:
                pieces.append((parts[1], lengths[1][1], size, ROW - size))
            lines.append((n, r, pieces))
    for i, acc in enumerate(accs):
        if fresh:
            acc[...] = jnp.zeros_like(acc)
        else:
            acc[...] = befores[i][...]
    for copy in note_copies:
        copy.wait()

    def note(n, r, k):
        return notes[n, r, k].astype(jnp.int32)

    def copies(m):
        return [
            pltpu.make_async_copy(
                part.at[pl.ds(frm, size)], held.at[m, pl.ds(to, size)], sem.at[2 * m + i]
            )
            for i, (part, frm, to, size) in enumerate(lines[m][2])
        ]

    for m, (n, r, _) in enumerate(lines):

        @pl.when(note(n, r, A_TILES) > 0)
        def _():
            for copy in copies(m):
                copy.start()

    for m, (n, r, _) in enumerate(lines):

        @pl.when(note(n, r, A_TILES) > 0)
        def _():
            for copy in copies(m):
                copy.wait()
            row = note(n, r, A_TILES) - 1
            cols = [note(n, r, k) - first[0] for k in range(A_TILES)]
            for k, c in enumerate(cols):
                h, l = halves(held[m, k * TILE : (k + 1) * TILE, :])
                left = jnp.concatenate([h, l], axis=1)
                t = jnp.dot(
                    left, jnp.concatenate([high[c], high[c]], axis=0), preferred_element_type=jnp.float32
                ) + jnp.dot(
                    left, jnp.concatenate([low[c], low[c]], axis=0), preferred_element_type=jnp.float32
                )
                h, l = halves(t)
                span = slice(k * P_TILES * TILE, (k + 1) * P_TILES * TILE)
                lifted[:TILE, span] = h
                lifted[TILE:, span] = l
            for p in range(P_TILES):
                for target, acc in zip(targets, accs):
                    mine = slots[rows + row, p] - 4 - 2 * target

                    @pl.when((mine == 0) | (mine == 1))
                    def _():
                        left = turned[row * P_TILES + p]
                        w = jnp.dot(
                            jnp.concatenate([left, left], axis=1), lifted[...], preferred_element_type=jnp.float32
                        )
                        w = w[:TILE] + w[TILE:]
                        for k, c in enumerate(cols):
                            for q in range(P_TILES):
                                lanes = (k * P_TILES + q) * TILE
                                s = mine * WIDTHS[target] + slots[c, q] - 2 * target
                                acc[s] += w[:, lanes : lanes + TILE]


def galerkin(weight, chunks, targets, first_row, slots, splits, befores, rows, coarse_rows):
    shapes = [tuple((x.shape[0], frm) for x, frm in parts) for parts in chunks]
    buffers = [x for parts in chunks for x, _ in parts]
    out = [jax.ShapeDtypeStruct((coarse_rows * WIDTHS[t], TILE, TILE), jnp.float32) for t in targets]
    befores = befores or []
    operands = [slots, first_row, *splits, *buffers, *befores]
    specs = [SMEM, SMEM] + [VMEM] * len(splits) + [ANY] * len(buffers) + [VMEM] * len(befores)
    lines = sum(min(CAP, -(-(parts[0][0] - META) // ROW)) for parts in shapes)
    return pl.pallas_call(
        functools.partial(galerkin_kernel, rows, shapes, targets, not befores),
        out_shape=out,
        in_specs=specs,
        out_specs=[VMEM] * len(out),
        scratch_shapes=[
            pltpu.VMEM((2 * TILE, A_TILES * P_TILES * TILE), jnp.bfloat16),
            pltpu.VMEM((lines, ROW, TILE), jnp.float32),
            pltpu.SMEM((len(chunks), META, TILE), jnp.float32),
            pltpu.SemaphoreType.DMA((len(chunks),)),
            pltpu.SemaphoreType.DMA((2 * lines,)),
        ],
        input_output_aliases={len(operands) - len(befores) + i: i for i in range(len(befores))},
        compiler_params=pltpu.CompilerParams(vmem_limit_bytes=20 * 2**20),
        cost_estimate=pl.CostEstimate(flops=weight, bytes_accessed=1, transcendentals=0),
        name="galerkin",
    )(*operands)


def after(value, *others):
    return lax.optimization_barrier((value, *others))[0]


def shards(a_tiles, a_cols, new_row, p_tiles, p_cols):
    rows = a_tiles.shape[0]
    coarse_rows = rows // 4
    my_x = lax.axis_index("gx").astype(jnp.int32)
    device = my_x * lax.axis_size("gy") + lax.axis_index("gy").astype(jnp.int32)

    p_here, send = buckets(a_tiles, a_cols, new_row, p_tiles, p_cols, my_x.reshape(1))
    p_before = beside(p_here, 1)
    p_after = beside(p_here, -1)
    sources = [p_before, p_here, p_after]
    d4 = hop(send["d4"], "gx", 4)
    far_a = hop(send["far_a"], "gx", -6)
    d3 = hop(after(send["d3"], p_after), "gx", 3)
    far_b = hop(after(send["far_b"], p_after), "gx", -6)
    d2 = hop(after(send["d2"], p_before, p_after), "gx", 2)

    slots = jnp.concatenate([x[-rows:, :P_TILES] for x in sources], axis=0).astype(jnp.int32)
    slots = slots - coarse_rows * device + 4
    splits = split(sources, rows)
    first_row = ((device - 1) * rows).reshape(1)

    def add(targets, chunks, befores, weight=1):
        return galerkin(weight, chunks, targets, first_row, slots, splits, befores, rows, coarse_rows)

    both = add((0, 1), [[(send["d0"], 0)]], None, 10**14)
    far_a = hop(after(far_a, p_before, p_after), "gx", -5)
    far_b = hop(after(far_b, both[0]), "gx", -5)
    d4 = after(d4, both[0])
    d1 = hop(after(send["d1"], d4), "gx", 1)
    both = add((0, 1), [[(d4, 0)]], both, 10**14)
    both = add((0, 1), [[(d3, 0)]], both)
    own, on = add((0, 1), [[(d2, 0)], [(far_a, 0)]], both)
    last = [[(d1, 0)], [(far_b, 0)]]
    (on,) = add((1,), last, [on])
    arrived = beside(on, 1)
    (own,) = add((0,), last, [own])
    own = own.reshape(coarse_rows, SLOTS, TILE, TILE)
    arrived = arrived.reshape(coarse_rows, WIDTHS[1], TILE, TILE)
    return own + jnp.pad(arrived, ((0, 0), (0, SLOTS - WIDTHS[1]), (0, 0), (0, 0)))


def solution(mesh):
    in_specs = (
        P(("gx", "gy"), None, None, None),
        P(("gx", "gy"), None),
        P(("gx", "gy")),
        P(("gx", "gy"), None, None, None),
        P(("gx", "gy"), None),
    )
    out_specs = P(("gx", "gy"), None, None, None)
    return jax.shard_map(shards, mesh=mesh, in_specs=in_specs, out_specs=out_specs, check_vma=False)
```

```python
import functools

import jax
import jax.numpy as jnp
from jax import lax
from jax.experimental import pallas as pl
from jax.experimental.pallas import tpu as pltpu
from jax.sharding import PartitionSpec as P

TILE = 128
A_TILES = 4
P_TILES = 2
CAP = 2
SPAN = 6
SLOTS = 10
ROW = A_TILES * TILE
META = 8
WIDTHS = (SLOTS, SLOTS - 2)

BUFFERS = {
    "far_a": (((10, 0, ROW),), True),
    "far_b": (((11, 0, ROW),), True),
    "d4": (((8, 0, ROW), (9, 0, ROW)), True),
    "d3": (((6, 0, ROW), (7, 0, ROW)), True),
    "d2": (((4, 0, ROW), (5, 0, ROW)), True),
    "d1": (((2, 0, ROW), (3, 0, ROW)), True),
    "d0": (((0, 0, ROW), (1, 0, ROW)), True),
}

ANY = pl.BlockSpec(memory_space=pl.ANY)
HBM = pl.BlockSpec(memory_space=pltpu.MemorySpace.HBM)
SMEM = pl.BlockSpec(memory_space=pltpu.SMEM)
VMEM = pl.BlockSpec(memory_space=pltpu.VMEM)


def hop(value, axis, steps):
    count = lax.axis_size(axis)
    return lax.ppermute(value, axis, [(i, (i + steps) % count) for i in range(count)])


def beside(value, steps):
    count = lax.axis_size("gy")
    route = [(i, i + steps) for i in range(count) if 0 <= i + steps < count]
    return lax.ppermute(value, "gy", route)


def bucket_kernel(rows, gx, per_x, layout, new_row, a_cols, p_cols, my_x, a_hbm, p_hbm, *refs):
    p_out, outs = refs[0], refs[1 : 1 + len(BUFFERS)]
    held, held_p, notes, order, in_sem, out_sem, note_sem, p_sem = refs[1 + len(BUFFERS) :]
    p_size = rows * P_TILES * TILE
    p_load = pltpu.make_async_copy(p_hbm, held_p.at[pl.ds(0, p_size)], p_sem)
    p_load.start()
    loads = [pltpu.make_async_copy(a_hbm.at[o], held.at[o], in_sem.at[o]) for o in range(rows)]
    for load in loads:
        load.start()
    for s in range(SPAN * CAP):
        order[s] = -1
    gaps = [lax.rem(lax.div(new_row[o], per_x) - my_x[0] + gx, gx) for o in range(rows)]
    for o in range(rows):
        rank = sum([(gaps[e] == gaps[o]).astype(jnp.int32) for e in range(o)], jnp.int32(0))
        order[gaps[o] * CAP + rank] = o
    lane = lax.broadcasted_iota(jnp.int32, (META, TILE), 1)
    line = lax.broadcasted_iota(jnp.int32, (META, TILE), 0)
    note_copies = []
    for b, (pieces, noted) in enumerate(layout):
        if not noted:
            continue
        note = jnp.zeros((META, TILE), jnp.int32)
        for r, (s, _, _) in enumerate(pieces):
            o = order[s]
            here = jnp.maximum(o, 0)
            place = jnp.where(o >= 0, lax.rem(new_row[here], rows) + 1, 0)
            for k in range(A_TILES):
                note = jnp.where((line == r) & (lane == k), a_cols[k, here], note)
            note = jnp.where((line == r) & (lane == A_TILES), place, note)
        notes[b] = note.astype(jnp.float32)
        size = sum(n for _, _, n in pieces)
        copy = pltpu.make_async_copy(notes.at[b], outs[b].at[pl.ds(size, META)], note_sem.at[b])
        copy.start()
        note_copies.append(copy)
    note = jnp.zeros((META, TILE), jnp.int32)
    for i in range(rows):
        for q in range(P_TILES):
            note = jnp.where((line == i) & (lane == q), p_cols[q, i], note)
    held_p[p_size:, :] = note.astype(jnp.float32)
    p_load.wait()
    p_copy = pltpu.make_async_copy(held_p, p_out, p_sem)
    p_copy.start()
    for load in loads:
        load.wait()

    def each(act):
        n = 0
        for out, (pieces, _) in zip(outs, layout):
            to = 0
            for s, frm, size in pieces:
                o = order[s]
                here = jnp.maximum(o, 0)

                @pl.when(o >= 0)
                def _():
                    act(
                        pltpu.make_async_copy(
                            held.at[here, pl.ds(frm, size)], out.at[pl.ds(to, size)], out_sem.at[n]
                        )
                    )

                to += size
                n += 1

    each(lambda copy: copy.start())
    each(lambda copy: copy.wait())
    for copy in note_copies:
        copy.wait()
    p_copy.wait()


def buckets(a_tiles, a_cols, new_row, p_tiles, p_cols, my_x):
    rows = a_tiles.shape[0]
    gx, gy = lax.axis_size("gx"), lax.axis_size("gy")
    layout = list(BUFFERS.values())
    lengths = [sum(n for _, _, n in pieces) + META * noted for pieces, noted in layout]
    p_lines = rows * P_TILES * TILE
    p_here, *outs = pl.pallas_call(
        functools.partial(bucket_kernel, rows, gx, rows * gy, layout),
        out_shape=[jax.ShapeDtypeStruct((n, TILE), jnp.float32) for n in [p_lines + META] + lengths],
        in_specs=[SMEM, SMEM, SMEM, SMEM, HBM, HBM],
        out_specs=[HBM] * (1 + len(lengths)),
        scratch_shapes=[
            pltpu.VMEM((rows, ROW, TILE), jnp.float32),
            pltpu.VMEM((p_lines + META, TILE), jnp.float32),
            pltpu.VMEM((len(lengths), META, TILE), jnp.float32),
            pltpu.SMEM((SPAN * CAP,), jnp.int32),
            pltpu.SemaphoreType.DMA((rows,)),
            pltpu.SemaphoreType.DMA((sum(len(p) for p, _ in layout),)),
            pltpu.SemaphoreType.DMA((len(lengths),)),
            pltpu.SemaphoreType.DMA,
        ],
        compiler_params=pltpu.CompilerParams(vmem_limit_bytes=60 * 2**20),
        name="buckets",
    )(new_row, a_cols.T, p_cols.T, my_x, a_tiles.reshape(rows, ROW, TILE), p_tiles.reshape(p_lines, TILE))
    return p_here, dict(zip(BUFFERS, outs))


def halves(x):
    high = x.astype(jnp.bfloat16)
    return high, (x - high.astype(jnp.float32)).astype(jnp.bfloat16)


def split_kernel(rows, *refs):
    sources, (high, low, turned) = refs[:3], refs[3:]
    for n, source in enumerate(sources):

        def body(i, carry):
            for q in range(P_TILES):
                block = source[pl.ds(pl.multiple_of((i * P_TILES + q) * TILE, TILE), TILE), :]
                h, l = halves(block)
                high[n * rows + i, :, q * TILE : (q + 1) * TILE] = h
                low[n * rows + i, :, q * TILE : (q + 1) * TILE] = l
                if n == 1:
                    h, l = halves(block.T)
                    turned[i * P_TILES + q, :TILE, :] = h
                    turned[i * P_TILES + q, TILE:, :] = l
            return carry

        lax.fori_loop(0, rows, body, 0)


def split(sources, rows):
    wide = jax.ShapeDtypeStruct((3 * rows, TILE, P_TILES * TILE), jnp.bfloat16)
    return pl.pallas_call(
        functools.partial(split_kernel, rows),
        out_shape=[wide, wide, jax.ShapeDtypeStruct((rows * P_TILES, 2 * TILE, TILE), jnp.bfloat16)],
        in_specs=[VMEM] * 3,
        out_specs=[VMEM] * 3,
        compiler_params=pltpu.CompilerParams(vmem_limit_bytes=12 * 2**20),
        name="split",
    )(*sources)


def galerkin_kernel(rows, chunks, targets, fresh, joined, slots, first, high, low, turned, *refs):
    buffers, refs = refs[: len(chunks)], refs[len(chunks) :]
    if not fresh:
        befores, refs = refs[: len(targets)], refs[len(targets) :]
    if joined:
        arrived, refs = refs[0], refs[1:]
    accs, refs = refs[: len(targets)], refs[len(targets) :]
    lifted, held, notes, note_sem, sem = refs
    note_copies, lines = [], []
    for n, (buffer, length) in enumerate(zip(buffers, chunks)):
        copy = pltpu.make_async_copy(buffer.at[pl.ds(length - META, META)], notes.at[n], note_sem.at[n])
        copy.start()
        note_copies.append(copy)
        lines += [(n, r) for r in range(length // ROW)]
    for i, acc in enumerate(accs):
        if fresh:
            acc[...] = jnp.zeros_like(acc)
        else:
            acc[...] = befores[i][...]
    if joined:
        for i in range(arrived.shape[0] // WIDTHS[1]):
            to = i * SLOTS
            acc[to : to + WIDTHS[1]] += arrived[i * WIDTHS[1] : (i + 1) * WIDTHS[1]]
    for copy in note_copies:
        copy.wait()

    def note(n, r, k):
        return notes[n, r, k].astype(jnp.int32)

    def fetch(m):
        n, r = lines[m]
        return pltpu.make_async_copy(buffers[n].at[pl.ds(r * ROW, ROW)], held.at[m], sem.at[m])

    for m, (n, r) in enumerate(lines):

        @pl.when(note(n, r, A_TILES) > 0)
        def _():
            fetch(m).start()

    for m, (n, r) in enumerate(lines):

        @pl.when(note(n, r, A_TILES) > 0)
        def _():
            fetch(m).wait()
            row = note(n, r, A_TILES) - 1
            cols = [note(n, r, k) - first[0] for k in range(A_TILES)]
            for k, c in enumerate(cols):
                h, l = halves(held[m, k * TILE : (k + 1) * TILE, :])
                left = jnp.concatenate([h, l], axis=1)
                t = jnp.dot(
                    left, jnp.concatenate([high[c], high[c]], axis=0), preferred_element_type=jnp.float32
                ) + jnp.dot(
                    left, jnp.concatenate([low[c], low[c]], axis=0), preferred_element_type=jnp.float32
                )
                h, l = halves(t)
                span = slice(k * P_TILES * TILE, (k + 1) * P_TILES * TILE)
                lifted[:TILE, span] = h
                lifted[TILE:, span] = l
            for p in range(P_TILES):
                for target, acc in zip(targets, accs):
                    mine = slots[rows + row, p] - 4 - 2 * target

                    @pl.when((mine == 0) | (mine == 1))
                    def _():
                        left = turned[row * P_TILES + p]
                        w = jnp.dot(
                            jnp.concatenate([left, left], axis=1), lifted[...], preferred_element_type=jnp.float32
                        )
                        w = w[:TILE] + w[TILE:]
                        for k, c in enumerate(cols):
                            for q in range(P_TILES):
                                lanes = (k * P_TILES + q) * TILE
                                s = mine * WIDTHS[target] + slots[c, q] - 2 * target
                                acc[s] += w[:, lanes : lanes + TILE]


def galerkin(weight, chunks, targets, first_row, slots, splits, befores, arrived, rows, coarse_rows):
    shapes = [x.shape[0] for x in chunks]
    out = [jax.ShapeDtypeStruct((coarse_rows * WIDTHS[t], TILE, TILE), jnp.float32) for t in targets]
    befores, joined = list(befores or []), [] if arrived is None else [arrived]
    operands = [slots, first_row, *splits, *chunks, *befores, *joined]
    specs = [SMEM, SMEM] + [VMEM] * len(splits) + [ANY] * len(chunks) + [VMEM] * len(befores + joined)
    lines = sum(n // ROW for n in shapes)
    return pl.pallas_call(
        functools.partial(galerkin_kernel, rows, shapes, targets, not befores, bool(joined)),
        out_shape=out,
        in_specs=specs,
        out_specs=[VMEM] * len(out),
        scratch_shapes=[
            pltpu.VMEM((2 * TILE, A_TILES * P_TILES * TILE), jnp.bfloat16),
            pltpu.VMEM((lines, ROW, TILE), jnp.float32),
            pltpu.SMEM((len(chunks), META, TILE), jnp.float32),
            pltpu.SemaphoreType.DMA((len(chunks),)),
            pltpu.SemaphoreType.DMA((lines,)),
        ],
        input_output_aliases={len(operands) - len(befores + joined) + i: i for i in range(len(befores))},
        compiler_params=pltpu.CompilerParams(vmem_limit_bytes=20 * 2**20),
        cost_estimate=pl.CostEstimate(flops=weight, bytes_accessed=1, transcendentals=0),
        name="galerkin",
    )(*operands)


def after(value, *others):
    return lax.optimization_barrier((value, *others))[0]


def pause_kernel(value, out):
    out[...] = value[...]


def pause(value):
    return pl.pallas_call(
        pause_kernel,
        out_shape=jax.ShapeDtypeStruct(value.shape, value.dtype),
        cost_estimate=pl.CostEstimate(flops=10**14, bytes_accessed=1, transcendentals=0),
        name="pause",
    )(value)


def shards(a_tiles, a_cols, new_row, p_tiles, p_cols):
    rows = a_tiles.shape[0]
    coarse_rows = rows // 4
    my_x = lax.axis_index("gx").astype(jnp.int32)
    device = my_x * lax.axis_size("gy") + lax.axis_index("gy").astype(jnp.int32)

    p_here, send = buckets(a_tiles, a_cols, new_row, p_tiles, p_cols, my_x.reshape(1))
    p_before = beside(p_here, 1)
    p_after = beside(p_here, -1)
    sources = [p_before, p_here, p_after]
    d4 = hop(send["d4"], "gx", 4)
    far_a = hop(send["far_a"], "gx", -6)
    far_b = hop(after(send["far_b"], p_after), "gx", -6)


    def tables(sources, middle):
        slots = jnp.concatenate([x[-rows:, :P_TILES] for x in sources], axis=0).astype(jnp.int32)
        slots = slots - coarse_rows * device + 4
        return ((middle - 1) * rows).reshape(1), slots, split(sources, rows)

    mine = tables([p_before, p_here, p_after], device)

    def add(data, targets, chunks, befores, weight=1, arrived=None):
        return galerkin(weight, chunks, targets, *data, befores, arrived, rows, coarse_rows)

    d3 = hop(after(send["d3"], p_after), "gx", 3)
    d2 = hop(after(send["d2"], p_before, p_after), "gx", 2)

    both = add(mine, (0, 1), [send["d0"]], None, 10**14)
    far_a = hop(after(far_a, both[0]), "gx", -5)
    p_before_2 = beside(after(p_before, both[0]), 1)
    theirs = tables([p_before_2, p_before, p_here], device - 1)
    d4 = after(d4, both[0])
    both = add(mine, (0, 1), [d4], both, 10**14)
    far_b = hop(after(far_b, both[0]), "gx", -5)
    d1 = hop(after(send["d1"], both[0]), "gx", 1)
    own, on = add(mine, (0, 1), [after(d3, theirs[1], *theirs[2])], both, 10**14)
    token = pause(on[0, :META])
    on = beside(on, 1)
    far_a, d2 = after(far_a, token), after(d2, token)

    f_far_a = beside(far_a, 1)
    f2 = beside(d2, 1)
    (own,) = add(mine, (0,), [d2, far_a], [own], 10**14)
    mid = own
    (own,) = add(theirs, (0,), [f2, f_far_a], [own], arrived=on)
    f1 = beside(after(d1, mid), 1)
    f_far_b = beside(after(far_b, mid), 1)
    (own,) = add(mine, (0,), [d1, far_b], [own], 10**14)
    (own,) = add(theirs, (0,), [f1, f_far_b], [own])
    return own.reshape(coarse_rows, SLOTS, TILE, TILE)


def solution(mesh):
    in_specs = (
        P(("gx", "gy"), None, None, None),
        P(("gx", "gy"), None),
        P(("gx", "gy")),
        P(("gx", "gy"), None, None, None),
        P(("gx", "gy"), None),
    )
    out_specs = P(("gx", "gy"), None, None, None)
    return jax.shard_map(shards, mesh=mesh, in_specs=in_specs, out_specs=out_specs, check_vma=False)
```

```python
import functools

import jax
import jax.numpy as jnp
from jax import lax
from jax.experimental import pallas as pl
from jax.experimental.pallas import tpu as pltpu
from jax.sharding import PartitionSpec as P

TILE = 128
A_TILES = 4
P_TILES = 2
CAP = 2
SPAN = 6
SLOTS = 10
ROW = A_TILES * TILE
META = 8
WIDTHS = (SLOTS, SLOTS - 2)

BUFFERS = {
    "far_a": (((10, 0, ROW),), True),
    "far_b": (((11, 0, ROW),), True),
    "d4": (((8, 0, ROW), (9, 0, ROW)), True),
    "d3": (((6, 0, ROW), (7, 0, ROW)), True),
    "d2": (((4, 0, ROW), (5, 0, ROW)), True),
    "d1": (((2, 0, ROW), (3, 0, ROW)), True),
    "d0": (((0, 0, ROW), (1, 0, ROW)), True),
}

ANY = pl.BlockSpec(memory_space=pl.ANY)
HBM = pl.BlockSpec(memory_space=pltpu.MemorySpace.HBM)
SMEM = pl.BlockSpec(memory_space=pltpu.SMEM)
VMEM = pl.BlockSpec(memory_space=pltpu.VMEM)


def hop(value, axis, steps):
    count = lax.axis_size(axis)
    return lax.ppermute(value, axis, [(i, (i + steps) % count) for i in range(count)])


def beside(value, steps):
    count = lax.axis_size("gy")
    route = [(i, i + steps) for i in range(count) if 0 <= i + steps < count]
    return lax.ppermute(value, "gy", route)


def bucket_kernel(rows, gx, per_x, layout, new_row, a_cols, p_cols, my_x, a_hbm, p_hbm, *refs):
    p_out, outs = refs[0], refs[1 : 1 + len(BUFFERS)]
    held, held_p, notes, order, in_sem, out_sem, note_sem, p_sem = refs[1 + len(BUFFERS) :]
    p_size = rows * P_TILES * TILE
    p_load = pltpu.make_async_copy(p_hbm, held_p.at[pl.ds(0, p_size)], p_sem)
    p_load.start()
    loads = [pltpu.make_async_copy(a_hbm.at[o], held.at[o], in_sem.at[o]) for o in range(rows)]
    for load in loads:
        load.start()
    for s in range(SPAN * CAP):
        order[s] = -1
    gaps = [lax.rem(lax.div(new_row[o], per_x) - my_x[0] + gx, gx) for o in range(rows)]
    for o in range(rows):
        rank = sum([(gaps[e] == gaps[o]).astype(jnp.int32) for e in range(o)], jnp.int32(0))
        order[gaps[o] * CAP + rank] = o
    lane = lax.broadcasted_iota(jnp.int32, (META, TILE), 1)
    line = lax.broadcasted_iota(jnp.int32, (META, TILE), 0)
    note_copies = []
    for b, (pieces, noted) in enumerate(layout):
        if not noted:
            continue
        note = jnp.zeros((META, TILE), jnp.int32)
        for r, (s, _, _) in enumerate(pieces):
            o = order[s]
            here = jnp.maximum(o, 0)
            place = jnp.where(o >= 0, lax.rem(new_row[here], rows) + 1, 0)
            for k in range(A_TILES):
                note = jnp.where((line == r) & (lane == k), a_cols[k, here], note)
            note = jnp.where((line == r) & (lane == A_TILES), place, note)
        notes[b] = note.astype(jnp.float32)
        size = sum(n for _, _, n in pieces)
        copy = pltpu.make_async_copy(notes.at[b], outs[b].at[pl.ds(size, META)], note_sem.at[b])
        copy.start()
        note_copies.append(copy)
    note = jnp.zeros((META, TILE), jnp.int32)
    for i in range(rows):
        for q in range(P_TILES):
            note = jnp.where((line == i) & (lane == q), p_cols[q, i], note)
    held_p[p_size:, :] = note.astype(jnp.float32)
    p_load.wait()
    p_copy = pltpu.make_async_copy(held_p, p_out, p_sem)
    p_copy.start()
    for load in loads:
        load.wait()

    def each(act):
        n = 0
        for out, (pieces, _) in zip(outs, layout):
            to = 0
            for s, frm, size in pieces:
                o = order[s]
                here = jnp.maximum(o, 0)

                @pl.when(o >= 0)
                def _():
                    act(
                        pltpu.make_async_copy(
                            held.at[here, pl.ds(frm, size)], out.at[pl.ds(to, size)], out_sem.at[n]
                        )
                    )

                to += size
                n += 1

    each(lambda copy: copy.start())
    each(lambda copy: copy.wait())
    for copy in note_copies:
        copy.wait()
    p_copy.wait()


def buckets(a_tiles, a_cols, new_row, p_tiles, p_cols, my_x):
    rows = a_tiles.shape[0]
    gx, gy = lax.axis_size("gx"), lax.axis_size("gy")
    layout = list(BUFFERS.values())
    lengths = [sum(n for _, _, n in pieces) + META * noted for pieces, noted in layout]
    p_lines = rows * P_TILES * TILE
    p_here, *outs = pl.pallas_call(
        functools.partial(bucket_kernel, rows, gx, rows * gy, layout),
        out_shape=[jax.ShapeDtypeStruct((n, TILE), jnp.float32) for n in [p_lines + META] + lengths],
        in_specs=[SMEM, SMEM, SMEM, SMEM, HBM, HBM],
        out_specs=[HBM] * (1 + len(lengths)),
        scratch_shapes=[
            pltpu.VMEM((rows, ROW, TILE), jnp.float32),
            pltpu.VMEM((p_lines + META, TILE), jnp.float32),
            pltpu.VMEM((len(lengths), META, TILE), jnp.float32),
            pltpu.SMEM((SPAN * CAP,), jnp.int32),
            pltpu.SemaphoreType.DMA((rows,)),
            pltpu.SemaphoreType.DMA((sum(len(p) for p, _ in layout),)),
            pltpu.SemaphoreType.DMA((len(lengths),)),
            pltpu.SemaphoreType.DMA,
        ],
        compiler_params=pltpu.CompilerParams(vmem_limit_bytes=60 * 2**20),
        name="buckets",
    )(new_row, a_cols.T, p_cols.T, my_x, a_tiles.reshape(rows, ROW, TILE), p_tiles.reshape(p_lines, TILE))
    return p_here, dict(zip(BUFFERS, outs))


def halves(x):
    high = x.astype(jnp.bfloat16)
    return high, (x - high.astype(jnp.float32)).astype(jnp.bfloat16)


def split_kernel(rows, *refs):
    sources, (high, low, turned) = refs[:3], refs[3:]
    for n, source in enumerate(sources):

        def body(i, carry):
            for q in range(P_TILES):
                block = source[pl.ds(pl.multiple_of((i * P_TILES + q) * TILE, TILE), TILE), :]
                h, l = halves(block)
                high[n * rows + i, :, q * TILE : (q + 1) * TILE] = h
                low[n * rows + i, :, q * TILE : (q + 1) * TILE] = l
                if n == 1:
                    h, l = halves(block.T)
                    turned[i * P_TILES + q, :TILE, :] = h
                    turned[i * P_TILES + q, TILE:, :] = l
            return carry

        lax.fori_loop(0, rows, body, 0)


def split(sources, rows):
    wide = jax.ShapeDtypeStruct((3 * rows, TILE, P_TILES * TILE), jnp.bfloat16)
    return pl.pallas_call(
        functools.partial(split_kernel, rows),
        out_shape=[wide, wide, jax.ShapeDtypeStruct((rows * P_TILES, 2 * TILE, TILE), jnp.bfloat16)],
        in_specs=[VMEM] * 3,
        out_specs=[VMEM] * 3,
        compiler_params=pltpu.CompilerParams(vmem_limit_bytes=12 * 2**20),
        name="split",
    )(*sources)


def galerkin_kernel(rows, chunks, targets, fresh, joined, slots, first, high, low, turned, *refs):
    buffers, refs = refs[: len(chunks)], refs[len(chunks) :]
    if not fresh:
        befores, refs = refs[: len(targets)], refs[len(targets) :]
    if joined:
        arrived, refs = refs[0], refs[1:]
    accs, refs = refs[: len(targets)], refs[len(targets) :]
    lifted, held, notes, note_sem, sem = refs
    note_copies, lines = [], []
    for n, (buffer, length) in enumerate(zip(buffers, chunks)):
        copy = pltpu.make_async_copy(buffer.at[pl.ds(length - META, META)], notes.at[n], note_sem.at[n])
        copy.start()
        note_copies.append(copy)
        lines += [(n, r) for r in range(length // ROW)]
    for i, acc in enumerate(accs):
        if fresh:
            acc[...] = jnp.zeros_like(acc)
        else:
            acc[...] = befores[i][...]
    if joined:
        for i in range(arrived.shape[0] // WIDTHS[1]):
            to = i * SLOTS
            acc[to : to + WIDTHS[1]] += arrived[i * WIDTHS[1] : (i + 1) * WIDTHS[1]]
    for copy in note_copies:
        copy.wait()

    def note(n, r, k):
        return notes[n, r, k].astype(jnp.int32)

    def fetch(m):
        n, r = lines[m]
        return pltpu.make_async_copy(buffers[n].at[pl.ds(r * ROW, ROW)], held.at[m], sem.at[m])

    for m, (n, r) in enumerate(lines):

        @pl.when(note(n, r, A_TILES) > 0)
        def _():
            fetch(m).start()

    for m, (n, r) in enumerate(lines):

        @pl.when(note(n, r, A_TILES) > 0)
        def _():
            fetch(m).wait()
            row = note(n, r, A_TILES) - 1
            cols = [note(n, r, k) - first[0] for k in range(A_TILES)]
            for k, c in enumerate(cols):
                h, l = halves(held[m, k * TILE : (k + 1) * TILE, :])
                left = jnp.concatenate([h, l], axis=1)
                t = jnp.dot(
                    left, jnp.concatenate([high[c], high[c]], axis=0), preferred_element_type=jnp.float32
                ) + jnp.dot(
                    left, jnp.concatenate([low[c], low[c]], axis=0), preferred_element_type=jnp.float32
                )
                h, l = halves(t)
                span = slice(k * P_TILES * TILE, (k + 1) * P_TILES * TILE)
                lifted[:TILE, span] = h
                lifted[TILE:, span] = l
            for p in range(P_TILES):
                for target, acc in zip(targets, accs):
                    mine = slots[rows + row, p] - 4 - 2 * target

                    @pl.when((mine == 0) | (mine == 1))
                    def _():
                        left = turned[row * P_TILES + p]
                        w = jnp.dot(
                            jnp.concatenate([left, left], axis=1), lifted[...], preferred_element_type=jnp.float32
                        )
                        w = w[:TILE] + w[TILE:]
                        for k, c in enumerate(cols):
                            for q in range(P_TILES):
                                lanes = (k * P_TILES + q) * TILE
                                s = mine * WIDTHS[target] + slots[c, q] - 2 * target
                                acc[s] += w[:, lanes : lanes + TILE]


def galerkin(weight, chunks, targets, first_row, slots, splits, befores, arrived, rows, coarse_rows):
    shapes = [x.shape[0] for x in chunks]
    out = [jax.ShapeDtypeStruct((coarse_rows * WIDTHS[t], TILE, TILE), jnp.float32) for t in targets]
    befores, joined = list(befores or []), [] if arrived is None else [arrived]
    operands = [slots, first_row, *splits, *chunks, *befores, *joined]
    specs = [SMEM, SMEM] + [VMEM] * len(splits) + [ANY] * len(chunks) + [VMEM] * len(befores + joined)
    lines = sum(n // ROW for n in shapes)
    return pl.pallas_call(
        functools.partial(galerkin_kernel, rows, shapes, targets, not befores, bool(joined)),
        out_shape=out,
        in_specs=specs,
        out_specs=[VMEM] * len(out),
        scratch_shapes=[
            pltpu.VMEM((2 * TILE, A_TILES * P_TILES * TILE), jnp.bfloat16),
            pltpu.VMEM((lines, ROW, TILE), jnp.float32),
            pltpu.SMEM((len(chunks), META, TILE), jnp.float32),
            pltpu.SemaphoreType.DMA((len(chunks),)),
            pltpu.SemaphoreType.DMA((lines,)),
        ],
        compiler_params=pltpu.CompilerParams(vmem_limit_bytes=20 * 2**20),
        cost_estimate=pl.CostEstimate(flops=weight, bytes_accessed=1, transcendentals=0),
        name="galerkin",
    )(*operands)


def after(value, *others):
    return lax.optimization_barrier((value, *others))[0]


def pause_kernel(value, out):
    out[...] = value[...]


def pause(value):
    return pl.pallas_call(
        pause_kernel,
        out_shape=jax.ShapeDtypeStruct(value.shape, value.dtype),
        cost_estimate=pl.CostEstimate(flops=10**14, bytes_accessed=1, transcendentals=0),
        name="pause",
    )(value)


def shards(a_tiles, a_cols, new_row, p_tiles, p_cols):
    rows = a_tiles.shape[0]
    coarse_rows = rows // 4
    my_x = lax.axis_index("gx").astype(jnp.int32)
    device = my_x * lax.axis_size("gy") + lax.axis_index("gy").astype(jnp.int32)

    p_here, send = buckets(a_tiles, a_cols, new_row, p_tiles, p_cols, my_x.reshape(1))
    p_before = beside(p_here, 1)
    p_after = beside(p_here, -1)
    sources = [p_before, p_here, p_after]
    d4 = hop(send["d4"], "gx", 4)
    far_a = hop(send["far_a"], "gx", -6)
    far_b = hop(after(send["far_b"], p_after), "gx", -6)


    def tables(sources, middle):
        slots = jnp.concatenate([x[-rows:, :P_TILES] for x in sources], axis=0).astype(jnp.int32)
        slots = slots - coarse_rows * device + 4
        return ((middle - 1) * rows).reshape(1), slots, split(sources, rows)

    mine = tables([p_before, p_here, p_after], device)

    def add(data, targets, chunks, befores, weight=1, arrived=None):
        return galerkin(weight, chunks, targets, *data, befores, arrived, rows, coarse_rows)

    d3 = hop(after(send["d3"], p_after), "gx", 3)
    d2 = hop(after(send["d2"], p_before, p_after), "gx", 2)

    both = add(mine, (0, 1), [send["d0"]], None, 10**14)
    far_a = hop(after(far_a, both[0]), "gx", -5)
    p_before_2 = beside(after(p_before, both[0]), 1)
    theirs = tables([p_before_2, p_before, p_here], device - 1)
    d4 = after(d4, both[0])
    both = add(mine, (0, 1), [d4], both, 10**14)
    far_b = hop(after(far_b, both[0]), "gx", -5)
    d1 = hop(after(send["d1"], both[0]), "gx", 1)
    own, on = add(mine, (0, 1), [after(d3, theirs[1], *theirs[2])], both, 10**14)
    token = pause(on[0, :META])
    on = beside(on, 1)
    far_a, d2 = after(far_a, token), after(d2, token)

    f_far_a = beside(far_a, 1)
    f2 = beside(d2, 1)
    (own,) = add(mine, (0,), [d2, far_a], [own], 10**14)
    mid = own
    (own,) = add(theirs, (0,), [f2, f_far_a], [own], arrived=on)
    f_far_b = beside(after(far_b, own), 1)
    f1 = beside(after(d1, mid), 1)
    (own,) = add(mine, (0,), [d1, far_b], [own], 10**14)
    (own,) = add(theirs, (0,), [f1, f_far_b], [own])
    return own.reshape(coarse_rows, SLOTS, TILE, TILE)


def solution(mesh):
    in_specs = (
        P(("gx", "gy"), None, None, None),
        P(("gx", "gy"), None),
        P(("gx", "gy")),
        P(("gx", "gy"), None, None, None),
        P(("gx", "gy"), None),
    )
    out_specs = P(("gx", "gy"), None, None, None)
    return jax.shard_map(shards, mesh=mesh, in_specs=in_specs, out_specs=out_specs, check_vma=False)
```

```python
import functools

import jax
import jax.numpy as jnp
from jax import lax
from jax.experimental import pallas as pl
from jax.experimental.pallas import tpu as pltpu
from jax.sharding import PartitionSpec as P

TILE = 128
A_TILES = 4
P_TILES = 2
CAP = 2
SPAN = 6
SLOTS = 10
ROW = A_TILES * TILE
META = 8
WIDTHS = (SLOTS, SLOTS - 2)

BUFFERS = {
    "far_a": (((10, 0, ROW),), True),
    "far_b": (((11, 0, ROW),), True),
    "d4": (((8, 0, ROW), (9, 0, ROW)), True),
    "d3": (((6, 0, ROW), (7, 0, ROW)), True),
    "d2": (((4, 0, ROW), (5, 0, ROW)), True),
    "d1": (((2, 0, ROW), (3, 0, ROW)), True),
    "d0": (((0, 0, ROW), (1, 0, ROW)), True),
}

ANY = pl.BlockSpec(memory_space=pl.ANY)
HBM = pl.BlockSpec(memory_space=pltpu.MemorySpace.HBM)
SMEM = pl.BlockSpec(memory_space=pltpu.SMEM)
VMEM = pl.BlockSpec(memory_space=pltpu.VMEM)


def hop(value, axis, steps):
    count = lax.axis_size(axis)
    return lax.ppermute(value, axis, [(i, (i + steps) % count) for i in range(count)])


def beside(value, steps):
    count = lax.axis_size("gy")
    route = [(i, i + steps) for i in range(count) if 0 <= i + steps < count]
    return lax.ppermute(value, "gy", route)


def bucket_kernel(rows, gx, per_x, layout, first, new_row, a_cols, p_cols, my_x, a_hbm, p_hbm, *refs):
    if first:
        p_out, refs = refs[0], refs[1:]
    outs, refs = refs[: len(layout)], refs[len(layout) :]
    held, held_p, notes, order, in_sem, out_sem, note_sem, p_sem = refs
    p_size = rows * P_TILES * TILE
    if first:
        p_load = pltpu.make_async_copy(p_hbm, held_p.at[pl.ds(0, p_size)], p_sem)
    loads = [pltpu.make_async_copy(a_hbm.at[o], held.at[o], in_sem.at[o]) for o in range(rows)]
    for s in range(SPAN * CAP):
        order[s] = -1
    gaps = [lax.rem(lax.div(new_row[o], per_x) - my_x[0] + gx, gx) for o in range(rows)]
    for o in range(rows):
        rank = sum([(gaps[e] == gaps[o]).astype(jnp.int32) for e in range(o)], jnp.int32(0))
        order[gaps[o] * CAP + rank] = o
    places = [s for pieces, _ in layout for s, _, _ in pieces]

    def wanted(o):
        return sum([(order[s] == o).astype(jnp.int32) for s in places]) > 0

    for o, load in enumerate(loads):

        @pl.when(wanted(o))
        def _():
            load.start()

    if first:
        p_load.start()
    lane = lax.broadcasted_iota(jnp.int32, (META, TILE), 1)
    line = lax.broadcasted_iota(jnp.int32, (META, TILE), 0)
    note_copies = []
    for b, (pieces, noted) in enumerate(layout):
        if not noted:
            continue
        note = jnp.zeros((META, TILE), jnp.int32)
        for r, (s, _, _) in enumerate(pieces):
            o = order[s]
            here = jnp.maximum(o, 0)
            place = jnp.where(o >= 0, lax.rem(new_row[here], rows) + 1, 0)
            for k in range(A_TILES):
                note = jnp.where((line == r) & (lane == k), a_cols[k, here], note)
            note = jnp.where((line == r) & (lane == A_TILES), place, note)
        notes[b] = note.astype(jnp.float32)
        size = sum(n for _, _, n in pieces)
        copy = pltpu.make_async_copy(notes.at[b], outs[b].at[pl.ds(size, META)], note_sem.at[b])
        copy.start()
        note_copies.append(copy)
    if first:
        note = jnp.zeros((META, TILE), jnp.int32)
        for i in range(rows):
            for q in range(P_TILES):
                note = jnp.where((line == i) & (lane == q), p_cols[q, i], note)
        held_p[p_size:, :] = note.astype(jnp.float32)
    for o, load in enumerate(loads):

        @pl.when(wanted(o))
        def _():
            load.wait()

    def each(act):
        n = 0
        for out, (pieces, _) in zip(outs, layout):
            to = 0
            for s, frm, size in pieces:
                o = order[s]
                here = jnp.maximum(o, 0)

                @pl.when(o >= 0)
                def _():
                    act(
                        pltpu.make_async_copy(
                            held.at[here, pl.ds(frm, size)], out.at[pl.ds(to, size)], out_sem.at[n]
                        )
                    )

                to += size
                n += 1

    each(lambda copy: copy.start())
    if first:
        p_load.wait()
        p_copy = pltpu.make_async_copy(held_p, p_out, p_sem)
        p_copy.start()
    each(lambda copy: copy.wait())
    for copy in note_copies:
        copy.wait()
    if first:
        p_copy.wait()


def buckets(names, a_tiles, a_cols, new_row, p_tiles, p_cols, my_x, first):
    rows = a_tiles.shape[0]
    gx, gy = lax.axis_size("gx"), lax.axis_size("gy")
    layout = [BUFFERS[name] for name in names]
    lengths = [sum(n for _, _, n in pieces) + META * noted for pieces, noted in layout]
    p_lines = rows * P_TILES * TILE
    outs = pl.pallas_call(
        functools.partial(bucket_kernel, rows, gx, rows * gy, layout, first),
        out_shape=[jax.ShapeDtypeStruct((n, TILE), jnp.float32) for n in [p_lines + META] * first + lengths],
        in_specs=[SMEM, SMEM, SMEM, SMEM, HBM, HBM],
        out_specs=[HBM] * (first + len(lengths)),
        scratch_shapes=[
            pltpu.VMEM((rows, ROW, TILE), jnp.float32),
            pltpu.VMEM((p_lines + META, TILE), jnp.float32),
            pltpu.VMEM((len(lengths), META, TILE), jnp.float32),
            pltpu.SMEM((SPAN * CAP,), jnp.int32),
            pltpu.SemaphoreType.DMA((rows,)),
            pltpu.SemaphoreType.DMA((sum(len(p) for p, _ in layout),)),
            pltpu.SemaphoreType.DMA((len(lengths),)),
            pltpu.SemaphoreType.DMA,
        ],
        compiler_params=pltpu.CompilerParams(vmem_limit_bytes=60 * 2**20),
        name="buckets",
    )(new_row, a_cols.T, p_cols.T, my_x, a_tiles.reshape(rows, ROW, TILE), p_tiles.reshape(p_lines, TILE))
    return dict(zip(["p"] * first + names, outs))


def halves(x):
    high = x.astype(jnp.bfloat16)
    return high, (x - high.astype(jnp.float32)).astype(jnp.bfloat16)


def split_kernel(rows, *refs):
    sources, (high, low, turned) = refs[:3], refs[3:]
    for n, source in enumerate(sources):

        def body(i, carry):
            for q in range(P_TILES):
                block = source[pl.ds(pl.multiple_of((i * P_TILES + q) * TILE, TILE), TILE), :]
                h, l = halves(block)
                high[n * rows + i, :, q * TILE : (q + 1) * TILE] = h
                low[n * rows + i, :, q * TILE : (q + 1) * TILE] = l
                if n == 1:
                    h, l = halves(block.T)
                    turned[i * P_TILES + q, :TILE, :] = h
                    turned[i * P_TILES + q, TILE:, :] = l
            return carry

        lax.fori_loop(0, rows, body, 0)


def split(sources, rows):
    wide = jax.ShapeDtypeStruct((3 * rows, TILE, P_TILES * TILE), jnp.bfloat16)
    return pl.pallas_call(
        functools.partial(split_kernel, rows),
        out_shape=[wide, wide, jax.ShapeDtypeStruct((rows * P_TILES, 2 * TILE, TILE), jnp.bfloat16)],
        in_specs=[VMEM] * 3,
        out_specs=[VMEM] * 3,
        compiler_params=pltpu.CompilerParams(vmem_limit_bytes=12 * 2**20),
        name="split",
    )(*sources)


def galerkin_kernel(rows, chunks, targets, fresh, joined, slots, first, high, low, turned, *refs):
    buffers, refs = refs[: len(chunks)], refs[len(chunks) :]
    if not fresh:
        befores, refs = refs[: len(targets)], refs[len(targets) :]
    if joined:
        arrived, refs = refs[0], refs[1:]
    accs, refs = refs[: len(targets)], refs[len(targets) :]
    lifted, held, notes, note_sem, sem = refs
    note_copies, lines = [], []
    for n, (buffer, length) in enumerate(zip(buffers, chunks)):
        copy = pltpu.make_async_copy(buffer.at[pl.ds(length - META, META)], notes.at[n], note_sem.at[n])
        copy.start()
        note_copies.append(copy)
        lines += [(n, r) for r in range(length // ROW)]
    def fetch(m):
        n, r = lines[m]
        return pltpu.make_async_copy(buffers[n].at[pl.ds(r * ROW, ROW)], held.at[m], sem.at[m])

    for m in range(len(lines)):
        fetch(m).start()
    for i, acc in enumerate(accs):
        if fresh:
            acc[...] = jnp.zeros_like(acc)
        else:
            acc[...] = befores[i][...]
    if joined:
        for i in range(arrived.shape[0] // WIDTHS[1]):
            to = i * SLOTS
            acc[to : to + WIDTHS[1]] += arrived[i * WIDTHS[1] : (i + 1) * WIDTHS[1]]
    for copy in note_copies:
        copy.wait()

    def note(n, r, k):
        return notes[n, r, k].astype(jnp.int32)

    for m, (n, r) in enumerate(lines):

        fetch(m).wait()

        @pl.when(note(n, r, A_TILES) > 0)
        def _():
            row = note(n, r, A_TILES) - 1
            cols = [note(n, r, k) - first[0] for k in range(A_TILES)]
            for k, c in enumerate(cols):
                h, l = halves(held[m, k * TILE : (k + 1) * TILE, :])
                left = jnp.concatenate([h, l], axis=1)
                t = jnp.dot(
                    left, jnp.concatenate([high[c], high[c]], axis=0), preferred_element_type=jnp.float32
                ) + jnp.dot(
                    left, jnp.concatenate([low[c], low[c]], axis=0), preferred_element_type=jnp.float32
                )
                h, l = halves(t)
                span = slice(k * P_TILES * TILE, (k + 1) * P_TILES * TILE)
                lifted[:TILE, span] = h
                lifted[TILE:, span] = l
            for p in range(P_TILES):
                for target, acc in zip(targets, accs):
                    mine = slots[rows + row, p] - 4 - 2 * target

                    @pl.when((mine == 0) | (mine == 1))
                    def _():
                        left = turned[row * P_TILES + p]
                        w = jnp.dot(
                            jnp.concatenate([left, left], axis=1), lifted[...], preferred_element_type=jnp.float32
                        )
                        w = w[:TILE] + w[TILE:]
                        for k, c in enumerate(cols):
                            for q in range(P_TILES):
                                lanes = (k * P_TILES + q) * TILE
                                s = mine * WIDTHS[target] + slots[c, q] - 2 * target
                                acc[s] += w[:, lanes : lanes + TILE]


def galerkin(weight, chunks, targets, first_row, slots, splits, befores, arrived, rows, coarse_rows):
    shapes = [x.shape[0] for x in chunks]
    out = [jax.ShapeDtypeStruct((coarse_rows * WIDTHS[t], TILE, TILE), jnp.float32) for t in targets]
    befores, joined = list(befores or []), [] if arrived is None else [arrived]
    operands = [slots, first_row, *splits, *chunks, *befores, *joined]
    specs = [SMEM, SMEM] + [VMEM] * len(splits) + [ANY] * len(chunks) + [VMEM] * len(befores + joined)
    lines = sum(n // ROW for n in shapes)
    return pl.pallas_call(
        functools.partial(galerkin_kernel, rows, shapes, targets, not befores, bool(joined)),
        out_shape=out,
        in_specs=specs,
        out_specs=[VMEM] * len(out),
        scratch_shapes=[
            pltpu.VMEM((2 * TILE, A_TILES * P_TILES * TILE), jnp.bfloat16),
            pltpu.VMEM((lines, ROW, TILE), jnp.float32),
            pltpu.SMEM((len(chunks), META, TILE), jnp.float32),
            pltpu.SemaphoreType.DMA((len(chunks),)),
            pltpu.SemaphoreType.DMA((lines,)),
        ],
        compiler_params=pltpu.CompilerParams(vmem_limit_bytes=20 * 2**20),
        cost_estimate=pl.CostEstimate(flops=weight, bytes_accessed=1, transcendentals=0),
        name="galerkin",
    )(*operands)


def after(value, *others):
    return lax.optimization_barrier((value, *others))[0]


def pause_kernel(value, out):
    out[...] = value[...]


def pause(value):
    return pl.pallas_call(
        pause_kernel,
        out_shape=jax.ShapeDtypeStruct(value.shape, value.dtype),
        cost_estimate=pl.CostEstimate(flops=10**14, bytes_accessed=1, transcendentals=0),
        name="pause",
    )(value)


def shards(a_tiles, a_cols, new_row, p_tiles, p_cols):
    rows = a_tiles.shape[0]
    coarse_rows = rows // 4
    my_x = lax.axis_index("gx").astype(jnp.int32)
    device = my_x * lax.axis_size("gy") + lax.axis_index("gy").astype(jnp.int32)

    operands = (a_cols, new_row, p_tiles, p_cols, my_x.reshape(1))
    send = buckets(["far_a", "d4"], a_tiles, *operands, True)
    p_here = send["p"]
    p_before = beside(p_here, 1)
    p_after = beside(p_here, -1)
    sources = [p_before, p_here, p_after]
    d4 = hop(send["d4"], "gx", 4)
    far_a = hop(send["far_a"], "gx", -6)
    send |= buckets(["far_b", "d3", "d2", "d1", "d0"], after(a_tiles, p_after), *operands, False)
    far_b = hop(after(send["far_b"], p_after), "gx", -6)


    def tables(sources, middle):
        slots = jnp.concatenate([x[-rows:, :P_TILES] for x in sources], axis=0).astype(jnp.int32)
        slots = slots - coarse_rows * device + 4
        return ((middle - 1) * rows).reshape(1), slots, split(sources, rows)

    mine = tables([p_before, p_here, p_after], device)

    def add(data, targets, chunks, befores, weight=1, arrived=None):
        return galerkin(weight, chunks, targets, *data, befores, arrived, rows, coarse_rows)

    d3 = hop(after(send["d3"], p_after), "gx", 3)
    d2 = hop(after(send["d2"], p_before, p_after), "gx", 2)

    both = add(mine, (0, 1), [send["d0"]], None, 10**14)
    far_a = hop(after(far_a, both[0]), "gx", -5)
    p_before_2 = beside(after(p_before, both[0]), 1)
    theirs = tables([p_before_2, p_before, p_here], device - 1)
    d4 = after(d4, both[0])
    both = add(mine, (0, 1), [d4], both, 10**14)
    far_b = hop(after(far_b, both[0]), "gx", -5)
    d1 = hop(after(send["d1"], both[0]), "gx", 1)
    own, on = add(mine, (0, 1), [after(d3, theirs[1], *theirs[2])], both, 10**14)
    token = pause(on[0, :META])
    on = beside(on, 1)
    far_a, d2 = after(far_a, token), after(d2, token)

    f_far_a = beside(far_a, 1)
    f2 = beside(d2, 1)
    (own,) = add(mine, (0,), [d2, far_a], [own], 10**14)
    mid = own
    (own,) = add(theirs, (0,), [f2, f_far_a], [own], arrived=on)
    f_far_b = beside(after(far_b, own), 1)
    f1 = beside(after(d1, mid), 1)
    (own,) = add(mine, (0,), [d1, far_b], [own], 10**14)
    (own,) = add(theirs, (0,), [f1, f_far_b], [own])
    return own.reshape(coarse_rows, SLOTS, TILE, TILE)


def solution(mesh):
    in_specs = (
        P(("gx", "gy"), None, None, None),
        P(("gx", "gy"), None),
        P(("gx", "gy")),
        P(("gx", "gy"), None, None, None),
        P(("gx", "gy"), None),
    )
    out_specs = P(("gx", "gy"), None, None, None)
    return jax.shard_map(shards, mesh=mesh, in_specs=in_specs, out_specs=out_specs, check_vma=False)
```

```python
import functools

import jax
import jax.numpy as jnp
from jax import lax
from jax.experimental import pallas as pl
from jax.experimental.pallas import tpu as pltpu
from jax.sharding import PartitionSpec as P

TILE = 128
A_TILES = 4
P_TILES = 2
CAP = 2
SPAN = 6
SLOTS = 10
ROW = A_TILES * TILE
META = 8
WIDTHS = (SLOTS, SLOTS - 2)

BUFFERS = {
    "far_a": (((10, 0, ROW),), True),
    "far_b": (((11, 0, ROW),), True),
    "d4": (((8, 0, ROW), (9, 0, ROW)), True),
    "d3": (((6, 0, ROW), (7, 0, ROW)), True),
    "d2": (((4, 0, ROW), (5, 0, ROW)), True),
    "d1": (((2, 0, ROW), (3, 0, ROW)), True),
    "d0": (((0, 0, ROW), (1, 0, ROW)), True),
}

ANY = pl.BlockSpec(memory_space=pl.ANY)
HBM = pl.BlockSpec(memory_space=pltpu.MemorySpace.HBM)
SMEM = pl.BlockSpec(memory_space=pltpu.SMEM)
VMEM = pl.BlockSpec(memory_space=pltpu.VMEM)


def hop(value, axis, steps):
    count = lax.axis_size(axis)
    return lax.ppermute(value, axis, [(i, (i + steps) % count) for i in range(count)])


def beside(value, steps):
    count = lax.axis_size("gy")
    route = [(i, i + steps) for i in range(count) if 0 <= i + steps < count]
    return lax.ppermute(value, "gy", route)


def bucket_kernel(rows, gx, per_x, layout, first, new_row, a_cols, p_cols, my_x, a_hbm, p_hbm, *refs):
    if first:
        p_out, refs = refs[0], refs[1:]
    outs, refs = refs[: len(layout)], refs[len(layout) :]
    held, held_p, notes, order, in_sem, out_sem, note_sem, p_sem = refs
    p_size = rows * P_TILES * TILE
    if first:
        p_load = pltpu.make_async_copy(p_hbm, held_p.at[pl.ds(0, p_size)], p_sem)
    loads = [pltpu.make_async_copy(a_hbm.at[o], held.at[o], in_sem.at[o]) for o in range(rows)]
    for s in range(SPAN * CAP):
        order[s] = -1
    gaps = [lax.rem(lax.div(new_row[o], per_x) - my_x[0] + gx, gx) for o in range(rows)]
    for o in range(rows):
        rank = sum([(gaps[e] == gaps[o]).astype(jnp.int32) for e in range(o)], jnp.int32(0))
        order[gaps[o] * CAP + rank] = o
    places = [s for pieces, _ in layout for s, _, _ in pieces]

    def wanted(o):
        return sum([(order[s] == o).astype(jnp.int32) for s in places]) > 0

    for o, load in enumerate(loads):

        @pl.when(wanted(o))
        def _():
            load.start()

    if first:
        p_load.start()
    lane = lax.broadcasted_iota(jnp.int32, (META, TILE), 1)
    line = lax.broadcasted_iota(jnp.int32, (META, TILE), 0)
    note_copies = []
    for b, (pieces, noted) in enumerate(layout):
        if not noted:
            continue
        note = jnp.zeros((META, TILE), jnp.int32)
        for r, (s, _, _) in enumerate(pieces):
            o = order[s]
            here = jnp.maximum(o, 0)
            place = jnp.where(o >= 0, lax.rem(new_row[here], rows) + 1, 0)
            for k in range(A_TILES):
                note = jnp.where((line == r) & (lane == k), a_cols[k, here], note)
            note = jnp.where((line == r) & (lane == A_TILES), place, note)
        notes[b] = note.astype(jnp.float32)
        size = sum(n for _, _, n in pieces)
        copy = pltpu.make_async_copy(notes.at[b], outs[b].at[pl.ds(size, META)], note_sem.at[b])
        copy.start()
        note_copies.append(copy)
    if first:
        note = jnp.zeros((META, TILE), jnp.int32)
        for i in range(rows):
            for q in range(P_TILES):
                note = jnp.where((line == i) & (lane == q), p_cols[q, i], note)
        held_p[p_size:, :] = note.astype(jnp.float32)
    for o, load in enumerate(loads):

        @pl.when(wanted(o))
        def _():
            load.wait()

    def each(act):
        n = 0
        for out, (pieces, _) in zip(outs, layout):
            to = 0
            for s, frm, size in pieces:
                o = order[s]
                here = jnp.maximum(o, 0)

                @pl.when(o >= 0)
                def _():
                    act(
                        pltpu.make_async_copy(
                            held.at[here, pl.ds(frm, size)], out.at[pl.ds(to, size)], out_sem.at[n]
                        )
                    )

                to += size
                n += 1

    each(lambda copy: copy.start())
    if first:
        p_load.wait()
        p_copy = pltpu.make_async_copy(held_p, p_out, p_sem)
        p_copy.start()
    each(lambda copy: copy.wait())
    for copy in note_copies:
        copy.wait()
    if first:
        p_copy.wait()


def buckets(names, a_tiles, a_cols, new_row, p_tiles, p_cols, my_x, first):
    rows = a_tiles.shape[0]
    gx, gy = lax.axis_size("gx"), lax.axis_size("gy")
    layout = [BUFFERS[name] for name in names]
    lengths = [sum(n for _, _, n in pieces) + META * noted for pieces, noted in layout]
    p_lines = rows * P_TILES * TILE
    outs = pl.pallas_call(
        functools.partial(bucket_kernel, rows, gx, rows * gy, layout, first),
        out_shape=[jax.ShapeDtypeStruct((n, TILE), jnp.float32) for n in [p_lines + META] * first + lengths],
        in_specs=[SMEM, SMEM, SMEM, SMEM, HBM, HBM],
        out_specs=[HBM] * (first + len(lengths)),
        scratch_shapes=[
            pltpu.VMEM((rows, ROW, TILE), jnp.float32),
            pltpu.VMEM((p_lines + META, TILE), jnp.float32),
            pltpu.VMEM((len(lengths), META, TILE), jnp.float32),
            pltpu.SMEM((SPAN * CAP,), jnp.int32),
            pltpu.SemaphoreType.DMA((rows,)),
            pltpu.SemaphoreType.DMA((sum(len(p) for p, _ in layout),)),
            pltpu.SemaphoreType.DMA((len(lengths),)),
            pltpu.SemaphoreType.DMA,
        ],
        compiler_params=pltpu.CompilerParams(vmem_limit_bytes=60 * 2**20),
        name="buckets",
    )(new_row, a_cols.T, p_cols.T, my_x, a_tiles.reshape(rows, ROW, TILE), p_tiles.reshape(p_lines, TILE))
    return dict(zip(["p"] * first + names, outs))


def halves(x):
    high = x.astype(jnp.bfloat16)
    return high, (x - high.astype(jnp.float32)).astype(jnp.bfloat16)


def split_kernel(rows, *refs):
    sources, (high, low, turned) = refs[:3], refs[3:]
    for n, source in enumerate(sources):

        def body(i, carry):
            for q in range(P_TILES):
                block = source[pl.ds(pl.multiple_of((i * P_TILES + q) * TILE, TILE), TILE), :]
                h, l = halves(block)
                high[n * rows + i, :, q * TILE : (q + 1) * TILE] = h
                low[n * rows + i, :, q * TILE : (q + 1) * TILE] = l
                if n == 1:
                    h, l = halves(block.T)
                    turned[i * P_TILES + q, :TILE, :] = h
                    turned[i * P_TILES + q, TILE:, :] = l
            return carry

        lax.fori_loop(0, rows, body, 0)


def split(sources, rows):
    wide = jax.ShapeDtypeStruct((3 * rows, TILE, P_TILES * TILE), jnp.bfloat16)
    return pl.pallas_call(
        functools.partial(split_kernel, rows),
        out_shape=[wide, wide, jax.ShapeDtypeStruct((rows * P_TILES, 2 * TILE, TILE), jnp.bfloat16)],
        in_specs=[VMEM] * 3,
        out_specs=[VMEM] * 3,
        compiler_params=pltpu.CompilerParams(vmem_limit_bytes=12 * 2**20),
        name="split",
    )(*sources)


def galerkin_kernel(rows, chunks, targets, fresh, joined, slots, first, high, low, turned, *refs):
    buffers, refs = refs[: len(chunks)], refs[len(chunks) :]
    if not fresh:
        befores, refs = refs[: len(targets)], refs[len(targets) :]
    if joined:
        arrived, refs = refs[0], refs[1:]
    accs, refs = refs[: len(targets)], refs[len(targets) :]
    lifted, held, notes, note_sem, sem = refs
    note_copies, lines = [], []
    for n, (buffer, length) in enumerate(zip(buffers, chunks)):
        copy = pltpu.make_async_copy(buffer.at[pl.ds(length - META, META)], notes.at[n], note_sem.at[n])
        copy.start()
        note_copies.append(copy)
        lines += [(n, r) for r in range(length // ROW)]
    def fetch(m):
        n, r = lines[m]
        return pltpu.make_async_copy(buffers[n].at[pl.ds(r * ROW, ROW)], held.at[m], sem.at[m])

    for m in range(len(lines)):
        fetch(m).start()
    for i, acc in enumerate(accs):
        if fresh:
            acc[...] = jnp.zeros_like(acc)
        else:
            acc[...] = befores[i][...]
    if joined:
        for i in range(arrived.shape[0] // WIDTHS[1]):
            to = i * SLOTS
            acc[to : to + WIDTHS[1]] += arrived[i * WIDTHS[1] : (i + 1) * WIDTHS[1]]
    for copy in note_copies:
        copy.wait()

    def note(n, r, k):
        return notes[n, r, k].astype(jnp.int32)

    for m, (n, r) in enumerate(lines):

        fetch(m).wait()

        @pl.when(note(n, r, A_TILES) > 0)
        def _():
            row = note(n, r, A_TILES) - 1
            cols = [note(n, r, k) - first[0] for k in range(A_TILES)]
            for k, c in enumerate(cols):
                h, l = halves(held[m, k * TILE : (k + 1) * TILE, :])
                left = jnp.concatenate([h, l], axis=1)
                t = jnp.dot(
                    left, jnp.concatenate([high[c], high[c]], axis=0), preferred_element_type=jnp.float32
                ) + jnp.dot(
                    left, jnp.concatenate([low[c], low[c]], axis=0), preferred_element_type=jnp.float32
                )
                h, l = halves(t)
                span = slice(k * P_TILES * TILE, (k + 1) * P_TILES * TILE)
                lifted[:TILE, span] = h
                lifted[TILE:, span] = l
            for p in range(P_TILES):
                for target, acc in zip(targets, accs):
                    mine = slots[rows + row, p] - 4 - 2 * target

                    @pl.when((mine == 0) | (mine == 1))
                    def _():
                        left = turned[row * P_TILES + p]
                        w = jnp.dot(
                            jnp.concatenate([left, left], axis=1), lifted[...], preferred_element_type=jnp.float32
                        )
                        w = w[:TILE] + w[TILE:]
                        for k, c in enumerate(cols):
                            for q in range(P_TILES):
                                lanes = (k * P_TILES + q) * TILE
                                s = mine * WIDTHS[target] + slots[c, q] - 2 * target
                                acc[s] += w[:, lanes : lanes + TILE]


def galerkin(weight, chunks, targets, first_row, slots, splits, befores, arrived, rows, coarse_rows):
    shapes = [x.shape[0] for x in chunks]
    out = [jax.ShapeDtypeStruct((coarse_rows * WIDTHS[t], TILE, TILE), jnp.float32) for t in targets]
    befores, joined = list(befores or []), [] if arrived is None else [arrived]
    operands = [slots, first_row, *splits, *chunks, *befores, *joined]
    specs = [SMEM, SMEM] + [VMEM] * len(splits) + [ANY] * len(chunks) + [VMEM] * len(befores + joined)
    lines = sum(n // ROW for n in shapes)
    return pl.pallas_call(
        functools.partial(galerkin_kernel, rows, shapes, targets, not befores, bool(joined)),
        out_shape=out,
        in_specs=specs,
        out_specs=[VMEM] * len(out),
        scratch_shapes=[
            pltpu.VMEM((2 * TILE, A_TILES * P_TILES * TILE), jnp.bfloat16),
            pltpu.VMEM((lines, ROW, TILE), jnp.float32),
            pltpu.SMEM((len(chunks), META, TILE), jnp.float32),
            pltpu.SemaphoreType.DMA((len(chunks),)),
            pltpu.SemaphoreType.DMA((lines,)),
        ],
        compiler_params=pltpu.CompilerParams(vmem_limit_bytes=20 * 2**20),
        cost_estimate=pl.CostEstimate(flops=weight, bytes_accessed=1, transcendentals=0),
        name="galerkin",
    )(*operands)


def after(value, *others):
    return lax.optimization_barrier((value, *others))[0]


def pause_kernel(value, out):
    out[...] = value[...]


def pause(value):
    return pl.pallas_call(
        pause_kernel,
        out_shape=jax.ShapeDtypeStruct(value.shape, value.dtype),
        cost_estimate=pl.CostEstimate(flops=10**14, bytes_accessed=1, transcendentals=0),
        name="pause",
    )(value)


def shards(a_tiles, a_cols, new_row, p_tiles, p_cols):
    rows = a_tiles.shape[0]
    coarse_rows = rows // 4
    my_x = lax.axis_index("gx").astype(jnp.int32)
    device = my_x * lax.axis_size("gy") + lax.axis_index("gy").astype(jnp.int32)

    operands = (a_cols, new_row, p_tiles, p_cols, my_x.reshape(1))
    send = buckets(["far_a", "d4"], a_tiles, *operands, True)
    p_here = send["p"]
    p_before = beside(p_here, 1)
    p_after = beside(p_here, -1)
    sources = [p_before, p_here, p_after]
    d4 = hop(send["d4"], "gx", 4)
    far_a = hop(send["far_a"], "gx", -6)
    send |= buckets(["far_b", "d3", "d2", "d1", "d0"], after(a_tiles, p_after), *operands, False)
    far_b = hop(after(send["far_b"], p_after), "gx", -6)


    def tables(sources, middle):
        slots = jnp.concatenate([x[-rows:, :P_TILES] for x in sources], axis=0).astype(jnp.int32)
        slots = slots - coarse_rows * device + 4
        return ((middle - 1) * rows).reshape(1), slots, split(sources, rows)

    mine = tables([p_before, p_here, p_after], device)

    def add(data, targets, chunks, befores, weight=1, arrived=None):
        return galerkin(weight, chunks, targets, *data, befores, arrived, rows, coarse_rows)

    d3 = hop(after(send["d3"], p_after), "gx", 3)
    d2 = hop(after(send["d2"], p_before, p_after), "gx", 2)

    both = add(mine, (0, 1), [send["d0"]], None, 10**14)
    far_a = hop(after(far_a, both[0]), "gx", -5)
    p_before_2 = beside(after(p_before, both[0]), 1)
    theirs = tables([p_before_2, p_before, p_here], device - 1)
    d4 = after(d4, both[0])
    both = add(mine, (0, 1), [d4], both, 10**14)
    far_b = hop(after(far_b, both[0]), "gx", -5)
    d1 = hop(after(send["d1"], both[0]), "gx", 1)
    own, on = add(mine, (0, 1), [after(d3, theirs[1], *theirs[2])], both, 10**14)
    token = pause(on[0, :META])
    on = beside(on, 1)
    far_a, d2 = after(far_a, token), after(d2, token)

    f_far_a = beside(far_a, 1)
    f2 = beside(d2, 1)
    (own,) = add(mine, (0,), [d2, far_a], [own], 10**14)
    mid = own
    token = pause(mid[0, :META])
    far_b = after(far_b, token)
    (own,) = add(theirs, (0,), [after(f2, token), f_far_a], [own], arrived=on)
    f1 = beside(after(d1, mid), 1)
    f_far_b = beside(far_b, 1)
    (own,) = add(mine, (0,), [d1, far_b], [own])
    (own,) = add(theirs, (0,), [f1, f_far_b], [own])
    return own.reshape(coarse_rows, SLOTS, TILE, TILE)


def solution(mesh):
    in_specs = (
        P(("gx", "gy"), None, None, None),
        P(("gx", "gy"), None),
        P(("gx", "gy")),
        P(("gx", "gy"), None, None, None),
        P(("gx", "gy"), None),
    )
    out_specs = P(("gx", "gy"), None, None, None)
    return jax.shard_map(shards, mesh=mesh, in_specs=in_specs, out_specs=out_specs, check_vma=False)
```

```python
import functools

import jax
import jax.numpy as jnp
from jax import lax
from jax.experimental import pallas as pl
from jax.experimental.pallas import tpu as pltpu
from jax.sharding import PartitionSpec as P

TILE = 128
A_TILES = 4
P_TILES = 2
CAP = 2
SPAN = 6
SLOTS = 10
ROW = A_TILES * TILE
META = 8
WIDTHS = (SLOTS, SLOTS - 2)

BUFFERS = {
    "far_a": (((10, 0, ROW),), True),
    "far_b": (((11, 0, ROW),), True),
    "d4": (((8, 0, ROW), (9, 0, ROW)), True),
    "d3": (((6, 0, ROW), (7, 0, ROW)), True),
    "d2": (((4, 0, ROW), (5, 0, ROW)), True),
    "d1": (((2, 0, ROW), (3, 0, ROW)), True),
    "d0": (((0, 0, ROW), (1, 0, ROW)), True),
}

ANY = pl.BlockSpec(memory_space=pl.ANY)
HBM = pl.BlockSpec(memory_space=pltpu.MemorySpace.HBM)
SMEM = pl.BlockSpec(memory_space=pltpu.SMEM)
VMEM = pl.BlockSpec(memory_space=pltpu.VMEM)


def hop(value, axis, steps):
    count = lax.axis_size(axis)
    return lax.ppermute(value, axis, [(i, (i + steps) % count) for i in range(count)])


def beside(value, steps):
    count = lax.axis_size("gy")
    route = [(i, i + steps) for i in range(count) if 0 <= i + steps < count]
    return lax.ppermute(value, "gy", route)


def bucket_kernel(rows, gx, per_x, layout, first, new_row, a_cols, p_cols, my_x, a_hbm, p_hbm, *refs):
    if first:
        p_out, refs = refs[0], refs[1:]
    outs, refs = refs[: len(layout)], refs[len(layout) :]
    held, held_p, notes, order, in_sem, out_sem, note_sem, p_sem = refs
    p_size = rows * P_TILES * TILE
    if first:
        p_load = pltpu.make_async_copy(p_hbm, held_p.at[pl.ds(0, p_size)], p_sem)
    loads = [pltpu.make_async_copy(a_hbm.at[o], held.at[o], in_sem.at[o]) for o in range(rows)]
    for s in range(SPAN * CAP):
        order[s] = -1
    gaps = [lax.rem(lax.div(new_row[o], per_x) - my_x[0] + gx, gx) for o in range(rows)]
    for o in range(rows):
        rank = sum([(gaps[e] == gaps[o]).astype(jnp.int32) for e in range(o)], jnp.int32(0))
        order[gaps[o] * CAP + rank] = o
    places = [s for pieces, _ in layout for s, _, _ in pieces]

    def wanted(o):
        return sum([(order[s] == o).astype(jnp.int32) for s in places]) > 0

    for o, load in enumerate(loads):

        @pl.when(wanted(o))
        def _():
            load.start()

    if first:
        p_load.start()
    lane = lax.broadcasted_iota(jnp.int32, (META, TILE), 1)
    line = lax.broadcasted_iota(jnp.int32, (META, TILE), 0)
    note_copies = []
    for b, (pieces, noted) in enumerate(layout):
        if not noted:
            continue
        note = jnp.zeros((META, TILE), jnp.int32)
        for r, (s, _, _) in enumerate(pieces):
            o = order[s]
            here = jnp.maximum(o, 0)
            place = jnp.where(o >= 0, lax.rem(new_row[here], rows) + 1, 0)
            for k in range(A_TILES):
                note = jnp.where((line == r) & (lane == k), a_cols[k, here], note)
            note = jnp.where((line == r) & (lane == A_TILES), place, note)
        notes[b] = note.astype(jnp.float32)
        size = sum(n for _, _, n in pieces)
        copy = pltpu.make_async_copy(notes.at[b], outs[b].at[pl.ds(size, META)], note_sem.at[b])
        copy.start()
        note_copies.append(copy)
    if first:
        note = jnp.zeros((META, TILE), jnp.int32)
        for i in range(rows):
            for q in range(P_TILES):
                note = jnp.where((line == i) & (lane == q), p_cols[q, i], note)
        held_p[p_size:, :] = note.astype(jnp.float32)
    for o, load in enumerate(loads):

        @pl.when(wanted(o))
        def _():
            load.wait()

    def each(act):
        n = 0
        for out, (pieces, _) in zip(outs, layout):
            to = 0
            for s, frm, size in pieces:
                o = order[s]
                here = jnp.maximum(o, 0)

                @pl.when(o >= 0)
                def _():
                    act(
                        pltpu.make_async_copy(
                            held.at[here, pl.ds(frm, size)], out.at[pl.ds(to, size)], out_sem.at[n]
                        )
                    )

                to += size
                n += 1

    each(lambda copy: copy.start())
    if first:
        p_load.wait()
        p_copy = pltpu.make_async_copy(held_p, p_out, p_sem)
        p_copy.start()
    each(lambda copy: copy.wait())
    for copy in note_copies:
        copy.wait()
    if first:
        p_copy.wait()


def buckets(names, a_tiles, a_cols, new_row, p_tiles, p_cols, my_x, first):
    rows = a_tiles.shape[0]
    gx, gy = lax.axis_size("gx"), lax.axis_size("gy")
    layout = [BUFFERS[name] for name in names]
    lengths = [sum(n for _, _, n in pieces) + META * noted for pieces, noted in layout]
    p_lines = rows * P_TILES * TILE
    outs = pl.pallas_call(
        functools.partial(bucket_kernel, rows, gx, rows * gy, layout, first),
        out_shape=[jax.ShapeDtypeStruct((n, TILE), jnp.float32) for n in [p_lines + META] * first + lengths],
        in_specs=[SMEM, SMEM, SMEM, SMEM, HBM, HBM],
        out_specs=[HBM] * (first + len(lengths)),
        scratch_shapes=[
            pltpu.VMEM((rows, ROW, TILE), jnp.float32),
            pltpu.VMEM((p_lines + META, TILE), jnp.float32),
            pltpu.VMEM((len(lengths), META, TILE), jnp.float32),
            pltpu.SMEM((SPAN * CAP,), jnp.int32),
            pltpu.SemaphoreType.DMA((rows,)),
            pltpu.SemaphoreType.DMA((sum(len(p) for p, _ in layout),)),
            pltpu.SemaphoreType.DMA((len(lengths),)),
            pltpu.SemaphoreType.DMA,
        ],
        compiler_params=pltpu.CompilerParams(vmem_limit_bytes=60 * 2**20),
        name="buckets",
    )(new_row, a_cols.T, p_cols.T, my_x, a_tiles.reshape(rows, ROW, TILE), p_tiles.reshape(p_lines, TILE))
    return dict(zip(["p"] * first + names, outs))


def halves(x):
    high = x.astype(jnp.bfloat16)
    return high, (x - high.astype(jnp.float32)).astype(jnp.bfloat16)


def split_kernel(rows, *refs):
    sources, (high, low, turned) = refs[:3], refs[3:]
    for n, source in enumerate(sources):

        def body(i, carry):
            for q in range(P_TILES):
                block = source[pl.ds(pl.multiple_of((i * P_TILES + q) * TILE, TILE), TILE), :]
                h, l = halves(block)
                high[n * rows + i, :, q * TILE : (q + 1) * TILE] = h
                low[n * rows + i, :, q * TILE : (q + 1) * TILE] = l
                if n == 1:
                    h, l = halves(block.T)
                    turned[i * P_TILES + q, :TILE, :] = h
                    turned[i * P_TILES + q, TILE:, :] = l
            return carry

        lax.fori_loop(0, rows, body, 0)


def split(sources, rows):
    wide = jax.ShapeDtypeStruct((3 * rows, TILE, P_TILES * TILE), jnp.bfloat16)
    return pl.pallas_call(
        functools.partial(split_kernel, rows),
        out_shape=[wide, wide, jax.ShapeDtypeStruct((rows * P_TILES, 2 * TILE, TILE), jnp.bfloat16)],
        in_specs=[VMEM] * 3,
        out_specs=[VMEM] * 3,
        compiler_params=pltpu.CompilerParams(vmem_limit_bytes=12 * 2**20),
        name="split",
    )(*sources)


def galerkin_kernel(rows, chunks, targets, fresh, joined, slots, first, high, low, turned, *refs):
    buffers, refs = refs[: len(chunks)], refs[len(chunks) :]
    if not fresh:
        befores, refs = refs[: len(targets)], refs[len(targets) :]
    if joined:
        arrived, refs = refs[0], refs[1:]
    accs, refs = refs[: len(targets)], refs[len(targets) :]
    lifted, held, notes, note_sem, sem = refs
    note_copies, lines = [], []
    for n, (buffer, length) in enumerate(zip(buffers, chunks)):
        copy = pltpu.make_async_copy(buffer.at[pl.ds(length - META, META)], notes.at[n], note_sem.at[n])
        copy.start()
        note_copies.append(copy)
        lines += [(n, r) for r in range(length // ROW)]
    def fetch(m):
        n, r = lines[m]
        return pltpu.make_async_copy(buffers[n].at[pl.ds(r * ROW, ROW)], held.at[m], sem.at[m])

    for m in range(len(lines)):
        fetch(m).start()
    for i, acc in enumerate(accs):
        if fresh:
            acc[...] = jnp.zeros_like(acc)
        else:
            acc[...] = befores[i][...]
    if joined:
        for i in range(arrived.shape[0] // WIDTHS[1]):
            to = i * SLOTS
            acc[to : to + WIDTHS[1]] += arrived[i * WIDTHS[1] : (i + 1) * WIDTHS[1]]
    for copy in note_copies:
        copy.wait()

    def note(n, r, k):
        return notes[n, r, k].astype(jnp.int32)

    for m, (n, r) in enumerate(lines):

        fetch(m).wait()

        @pl.when(note(n, r, A_TILES) > 0)
        def _():
            row = note(n, r, A_TILES) - 1
            cols = [note(n, r, k) - first[0] for k in range(A_TILES)]
            for k, c in enumerate(cols):
                h, l = halves(held[m, k * TILE : (k + 1) * TILE, :])
                left = jnp.concatenate([h, l], axis=1)
                t = jnp.dot(
                    left, jnp.concatenate([high[c], high[c]], axis=0), preferred_element_type=jnp.float32
                ) + jnp.dot(
                    left, jnp.concatenate([low[c], low[c]], axis=0), preferred_element_type=jnp.float32
                )
                h, l = halves(t)
                span = slice(k * P_TILES * TILE, (k + 1) * P_TILES * TILE)
                lifted[:TILE, span] = h
                lifted[TILE:, span] = l
            for p in range(P_TILES):
                for target, acc in zip(targets, accs):
                    mine = slots[rows + row, p] - 4 - 2 * target

                    @pl.when((mine == 0) | (mine == 1))
                    def _():
                        left = turned[row * P_TILES + p]
                        w = jnp.dot(
                            jnp.concatenate([left, left], axis=1), lifted[...], preferred_element_type=jnp.float32
                        )
                        w = w[:TILE] + w[TILE:]
                        for k, c in enumerate(cols):
                            for q in range(P_TILES):
                                lanes = (k * P_TILES + q) * TILE
                                s = mine * WIDTHS[target] + slots[c, q] - 2 * target
                                acc[s] += w[:, lanes : lanes + TILE]


def galerkin(weight, chunks, targets, first_row, slots, splits, befores, arrived, rows, coarse_rows):
    shapes = [x.shape[0] for x in chunks]
    out = [jax.ShapeDtypeStruct((coarse_rows * WIDTHS[t], TILE, TILE), jnp.float32) for t in targets]
    befores, joined = list(befores or []), [] if arrived is None else [arrived]
    operands = [slots, first_row, *splits, *chunks, *befores, *joined]
    specs = [SMEM, SMEM] + [VMEM] * len(splits) + [ANY] * len(chunks) + [VMEM] * len(befores + joined)
    lines = sum(n // ROW for n in shapes)
    return pl.pallas_call(
        functools.partial(galerkin_kernel, rows, shapes, targets, not befores, bool(joined)),
        out_shape=out,
        in_specs=specs,
        out_specs=[VMEM] * len(out),
        scratch_shapes=[
            pltpu.VMEM((2 * TILE, A_TILES * P_TILES * TILE), jnp.bfloat16),
            pltpu.VMEM((lines, ROW, TILE), jnp.float32),
            pltpu.SMEM((len(chunks), META, TILE), jnp.float32),
            pltpu.SemaphoreType.DMA((len(chunks),)),
            pltpu.SemaphoreType.DMA((lines,)),
        ],
        compiler_params=pltpu.CompilerParams(vmem_limit_bytes=20 * 2**20),
        cost_estimate=pl.CostEstimate(flops=weight, bytes_accessed=1, transcendentals=0),
        name="galerkin",
    )(*operands)


def after(value, *others):
    return lax.optimization_barrier((value, *others))[0]


def pause_kernel(value, out):
    out[...] = value[...]


def pause(value):
    return pl.pallas_call(
        pause_kernel,
        out_shape=jax.ShapeDtypeStruct(value.shape, value.dtype),
        cost_estimate=pl.CostEstimate(flops=10**14, bytes_accessed=1, transcendentals=0),
        name="pause",
    )(value)


def shards(a_tiles, a_cols, new_row, p_tiles, p_cols):
    rows = a_tiles.shape[0]
    coarse_rows = rows // 4
    my_x = lax.axis_index("gx").astype(jnp.int32)
    device = my_x * lax.axis_size("gy") + lax.axis_index("gy").astype(jnp.int32)

    operands = (a_cols, new_row, p_tiles, p_cols, my_x.reshape(1))
    send = buckets(["far_a", "d4"], a_tiles, *operands, True)
    p_here = send["p"]
    p_before = beside(p_here, 1)
    p_after = beside(p_here, -1)
    sources = [p_before, p_here, p_after]
    d4 = hop(send["d4"], "gx", 4)
    far_a = hop(send["far_a"], "gx", -6)
    send |= buckets(["far_b", "d3", "d2", "d1", "d0"], after(a_tiles, p_after), *operands, False)
    far_b = hop(after(send["far_b"], p_after), "gx", -6)


    def tables(sources, middle):
        slots = jnp.concatenate([x[-rows:, :P_TILES] for x in sources], axis=0).astype(jnp.int32)
        slots = slots - coarse_rows * device + 4
        return ((middle - 1) * rows).reshape(1), slots, split(sources, rows)

    mine = tables([p_before, p_here, p_after], device)

    def add(data, targets, chunks, befores, weight=1, arrived=None):
        return galerkin(weight, chunks, targets, *data, befores, arrived, rows, coarse_rows)

    d3 = hop(after(send["d3"], p_after), "gx", 3)
    d2 = hop(after(send["d2"], p_before, p_after), "gx", 2)

    both = add(mine, (0, 1), [send["d0"]], None, 10**14)
    far_a = hop(after(far_a, both[0]), "gx", -5)
    p_before_2 = beside(after(p_before, both[0]), 1)
    theirs = tables([p_before_2, p_before, p_here], device - 1)
    d4 = after(d4, both[0])
    both = add(mine, (0, 1), [d4], both, 10**14)
    far_b = hop(after(far_b, both[0]), "gx", -5)
    d1 = hop(after(send["d1"], both[0]), "gx", 1)
    own, on = add(mine, (0, 1), [after(d3, theirs[1], *theirs[2])], both, 10**14)
    token = pause(on[0, :META])
    on = beside(on, 1)
    far_a, d2 = after(far_a, token), after(d2, token)

    f_far_a = beside(far_a, 1)
    f2 = beside(d2, 1)
    (own,) = add(mine, (0,), [d2, far_a], [own], 10**14)
    mid = own
    (own,) = add(theirs, (0,), [f2, f_far_a], [own], arrived=on)
    f1 = beside(after(d1, mid), 1)
    f_far_b = beside(after(far_b, mid, d1), 1)
    (own,) = add(mine, (0,), [d1, far_b], [own])
    (own,) = add(theirs, (0,), [f1, f_far_b], [own])
    return own.reshape(coarse_rows, SLOTS, TILE, TILE)


def solution(mesh):
    in_specs = (
        P(("gx", "gy"), None, None, None),
        P(("gx", "gy"), None),
        P(("gx", "gy")),
        P(("gx", "gy"), None, None, None),
        P(("gx", "gy"), None),
    )
    out_specs = P(("gx", "gy"), None, None, None)
    return jax.shard_map(shards, mesh=mesh, in_specs=in_specs, out_specs=out_specs, check_vma=False)
```

```python
import functools

import jax
import jax.numpy as jnp
from jax import lax
from jax.experimental import pallas as pl
from jax.experimental.pallas import tpu as pltpu
from jax.sharding import PartitionSpec as P

TILE = 128
A_TILES = 4
P_TILES = 2
CAP = 2
SPAN = 6
SLOTS = 10
ROW = A_TILES * TILE
META = 8
WIDTHS = (SLOTS, SLOTS - 2)

BUFFERS = {
    "far_a": (((10, 0, ROW),), True),
    "far_b": (((11, 0, ROW),), True),
    "d4": (((8, 0, ROW), (9, 0, ROW)), True),
    "d3": (((6, 0, ROW), (7, 0, ROW)), True),
    "d2": (((4, 0, ROW), (5, 0, ROW)), True),
    "d1": (((2, 0, ROW), (3, 0, ROW)), True),
    "d0": (((0, 0, ROW), (1, 0, ROW)), True),
}

ANY = pl.BlockSpec(memory_space=pl.ANY)
HBM = pl.BlockSpec(memory_space=pltpu.MemorySpace.HBM)
SMEM = pl.BlockSpec(memory_space=pltpu.SMEM)
VMEM = pl.BlockSpec(memory_space=pltpu.VMEM)


def hop(value, axis, steps):
    count = lax.axis_size(axis)
    return lax.ppermute(value, axis, [(i, (i + steps) % count) for i in range(count)])


def beside(value, steps):
    count = lax.axis_size("gy")
    route = [(i, i + steps) for i in range(count) if 0 <= i + steps < count]
    return lax.ppermute(value, "gy", route)


def bucket_kernel(rows, gx, per_x, layout, first, new_row, a_cols, p_cols, my_x, a_hbm, p_hbm, *refs):
    if first:
        p_out, refs = refs[0], refs[1:]
    outs, refs = refs[: len(layout)], refs[len(layout) :]
    held, held_p, notes, order, in_sem, out_sem, note_sem, p_sem = refs
    p_size = rows * P_TILES * TILE
    if first:
        p_load = pltpu.make_async_copy(p_hbm, held_p.at[pl.ds(0, p_size)], p_sem)
    loads = [pltpu.make_async_copy(a_hbm.at[o], held.at[o], in_sem.at[o]) for o in range(rows)]
    for s in range(SPAN * CAP):
        order[s] = -1
    gaps = [lax.rem(lax.div(new_row[o], per_x) - my_x[0] + gx, gx) for o in range(rows)]
    for o in range(rows):
        rank = sum([(gaps[e] == gaps[o]).astype(jnp.int32) for e in range(o)], jnp.int32(0))
        order[gaps[o] * CAP + rank] = o
    places = [s for pieces, _ in layout for s, _, _ in pieces]

    def wanted(o):
        return sum([(order[s] == o).astype(jnp.int32) for s in places]) > 0

    for o, load in enumerate(loads):

        @pl.when(wanted(o))
        def _():
            load.start()

    if first:
        p_load.start()
    lane = lax.broadcasted_iota(jnp.int32, (META, TILE), 1)
    line = lax.broadcasted_iota(jnp.int32, (META, TILE), 0)
    note_copies = []
    for b, (pieces, noted) in enumerate(layout):
        if not noted:
            continue
        note = jnp.zeros((META, TILE), jnp.int32)
        for r, (s, _, _) in enumerate(pieces):
            o = order[s]
            here = jnp.maximum(o, 0)
            place = jnp.where(o >= 0, lax.rem(new_row[here], rows) + 1, 0)
            for k in range(A_TILES):
                note = jnp.where((line == r) & (lane == k), a_cols[k, here], note)
            note = jnp.where((line == r) & (lane == A_TILES), place, note)
        notes[b] = note.astype(jnp.float32)
        size = sum(n for _, _, n in pieces)
        copy = pltpu.make_async_copy(notes.at[b], outs[b].at[pl.ds(size, META)], note_sem.at[b])
        copy.start()
        note_copies.append(copy)
    if first:
        note = jnp.zeros((META, TILE), jnp.int32)
        for i in range(rows):
            for q in range(P_TILES):
                note = jnp.where((line == i) & (lane == q), p_cols[q, i], note)
        held_p[p_size:, :] = note.astype(jnp.float32)
    for o, load in enumerate(loads):

        @pl.when(wanted(o))
        def _():
            load.wait()

    def each(act):
        n = 0
        for out, (pieces, _) in zip(outs, layout):
            to = 0
            for s, frm, size in pieces:
                o = order[s]
                here = jnp.maximum(o, 0)

                @pl.when(o >= 0)
                def _():
                    act(
                        pltpu.make_async_copy(
                            held.at[here, pl.ds(frm, size)], out.at[pl.ds(to, size)], out_sem.at[n]
                        )
                    )

                to += size
                n += 1

    each(lambda copy: copy.start())
    if first:
        p_load.wait()
        p_copy = pltpu.make_async_copy(held_p, p_out, p_sem)
        p_copy.start()
    each(lambda copy: copy.wait())
    for copy in note_copies:
        copy.wait()
    if first:
        p_copy.wait()


def buckets(names, a_tiles, a_cols, new_row, p_tiles, p_cols, my_x, first):
    rows = a_tiles.shape[0]
    gx, gy = lax.axis_size("gx"), lax.axis_size("gy")
    layout = [BUFFERS[name] for name in names]
    lengths = [sum(n for _, _, n in pieces) + META * noted for pieces, noted in layout]
    p_lines = rows * P_TILES * TILE
    outs = pl.pallas_call(
        functools.partial(bucket_kernel, rows, gx, rows * gy, layout, first),
        out_shape=[jax.ShapeDtypeStruct((n, TILE), jnp.float32) for n in [p_lines + META] * first + lengths],
        in_specs=[SMEM, SMEM, SMEM, SMEM, HBM, HBM],
        out_specs=[HBM] * (first + len(lengths)),
        scratch_shapes=[
            pltpu.VMEM((rows, ROW, TILE), jnp.float32),
            pltpu.VMEM((p_lines + META, TILE), jnp.float32),
            pltpu.VMEM((len(lengths), META, TILE), jnp.float32),
            pltpu.SMEM((SPAN * CAP,), jnp.int32),
            pltpu.SemaphoreType.DMA((rows,)),
            pltpu.SemaphoreType.DMA((sum(len(p) for p, _ in layout),)),
            pltpu.SemaphoreType.DMA((len(lengths),)),
            pltpu.SemaphoreType.DMA,
        ],
        compiler_params=pltpu.CompilerParams(vmem_limit_bytes=60 * 2**20),
        name="buckets",
    )(new_row, a_cols.T, p_cols.T, my_x, a_tiles.reshape(rows, ROW, TILE), p_tiles.reshape(p_lines, TILE))
    return dict(zip(["p"] * first + names, outs))


def halves(x):
    high = x.astype(jnp.bfloat16)
    return high, (x - high.astype(jnp.float32)).astype(jnp.bfloat16)


def split_kernel(rows, *refs):
    sources, (high, low, turned) = refs[:3], refs[3:]
    for n, source in enumerate(sources):

        def body(i, carry):
            for q in range(P_TILES):
                block = source[pl.ds(pl.multiple_of((i * P_TILES + q) * TILE, TILE), TILE), :]
                h, l = halves(block)
                high[n * rows + i, :, q * TILE : (q + 1) * TILE] = h
                low[n * rows + i, :, q * TILE : (q + 1) * TILE] = l
                if n == 1:
                    h, l = halves(block.T)
                    turned[i * P_TILES + q, :TILE, :] = h
                    turned[i * P_TILES + q, TILE:, :] = l
            return carry

        lax.fori_loop(0, rows, body, 0)


def split(sources, rows):
    wide = jax.ShapeDtypeStruct((3 * rows, TILE, P_TILES * TILE), jnp.bfloat16)
    return pl.pallas_call(
        functools.partial(split_kernel, rows),
        out_shape=[wide, wide, jax.ShapeDtypeStruct((rows * P_TILES, 2 * TILE, TILE), jnp.bfloat16)],
        in_specs=[VMEM] * 3,
        out_specs=[VMEM] * 3,
        compiler_params=pltpu.CompilerParams(vmem_limit_bytes=12 * 2**20),
        name="split",
    )(*sources)


def galerkin_kernel(rows, chunks, targets, fresh, joined, slots, first, high, low, turned, *refs):
    buffers, refs = refs[: len(chunks)], refs[len(chunks) :]
    if not fresh:
        befores, refs = refs[: len(targets)], refs[len(targets) :]
    if joined:
        arrived, refs = refs[0], refs[1:]
    accs, refs = refs[: len(targets)], refs[len(targets) :]
    lifted, held, notes, note_sem, sem = refs
    note_copies, lines = [], []
    for n, (buffer, length) in enumerate(zip(buffers, chunks)):
        copy = pltpu.make_async_copy(buffer.at[pl.ds(length - META, META)], notes.at[n], note_sem.at[n])
        copy.start()
        note_copies.append(copy)
        lines += [(n, r) for r in range(length // ROW)]
    def fetch(m):
        n, r = lines[m]
        return pltpu.make_async_copy(buffers[n].at[pl.ds(r * ROW, ROW)], held.at[m], sem.at[m])

    for m in range(len(lines)):
        fetch(m).start()
    for i, acc in enumerate(accs):
        if fresh:
            acc[...] = jnp.zeros_like(acc)
        else:
            acc[...] = befores[i][...]
    if joined:
        for i in range(arrived.shape[0] // WIDTHS[1]):
            to = i * SLOTS
            acc[to : to + WIDTHS[1]] += arrived[i * WIDTHS[1] : (i + 1) * WIDTHS[1]]
    for copy in note_copies:
        copy.wait()

    def note(n, r, k):
        return notes[n, r, k].astype(jnp.int32)

    for m, (n, r) in enumerate(lines):

        fetch(m).wait()

        @pl.when(note(n, r, A_TILES) > 0)
        def _():
            row = note(n, r, A_TILES) - 1
            cols = [note(n, r, k) - first[0] for k in range(A_TILES)]
            for k, c in enumerate(cols):
                h, l = halves(held[m, k * TILE : (k + 1) * TILE, :])
                left = jnp.concatenate([h, l], axis=1)
                t = jnp.dot(
                    left, jnp.concatenate([high[c], high[c]], axis=0), preferred_element_type=jnp.float32
                ) + jnp.dot(
                    left, jnp.concatenate([low[c], low[c]], axis=0), preferred_element_type=jnp.float32
                )
                h, l = halves(t)
                span = slice(k * P_TILES * TILE, (k + 1) * P_TILES * TILE)
                lifted[:TILE, span] = h
                lifted[TILE:, span] = l
            for p in range(P_TILES):
                for target, acc in zip(targets, accs):
                    mine = slots[rows + row, p] - 4 - 2 * target

                    @pl.when((mine == 0) | (mine == 1))
                    def _():
                        left = turned[row * P_TILES + p]
                        w = jnp.dot(
                            jnp.concatenate([left, left], axis=1), lifted[...], preferred_element_type=jnp.float32
                        )
                        w = w[:TILE] + w[TILE:]
                        for k, c in enumerate(cols):
                            for q in range(P_TILES):
                                lanes = (k * P_TILES + q) * TILE
                                s = mine * WIDTHS[target] + slots[c, q] - 2 * target
                                acc[s] += w[:, lanes : lanes + TILE]


def galerkin(weight, chunks, targets, first_row, slots, splits, befores, arrived, rows, coarse_rows):
    shapes = [x.shape[0] for x in chunks]
    out = [jax.ShapeDtypeStruct((coarse_rows * WIDTHS[t], TILE, TILE), jnp.float32) for t in targets]
    befores, joined = list(befores or []), [] if arrived is None else [arrived]
    operands = [slots, first_row, *splits, *chunks, *befores, *joined]
    specs = [SMEM, SMEM] + [VMEM] * len(splits) + [ANY] * len(chunks) + [VMEM] * len(befores + joined)
    lines = sum(n // ROW for n in shapes)
    return pl.pallas_call(
        functools.partial(galerkin_kernel, rows, shapes, targets, not befores, bool(joined)),
        out_shape=out,
        in_specs=specs,
        out_specs=[VMEM] * len(out),
        scratch_shapes=[
            pltpu.VMEM((2 * TILE, A_TILES * P_TILES * TILE), jnp.bfloat16),
            pltpu.VMEM((lines, ROW, TILE), jnp.float32),
            pltpu.SMEM((len(chunks), META, TILE), jnp.float32),
            pltpu.SemaphoreType.DMA((len(chunks),)),
            pltpu.SemaphoreType.DMA((lines,)),
        ],
        compiler_params=pltpu.CompilerParams(vmem_limit_bytes=20 * 2**20),
        cost_estimate=pl.CostEstimate(flops=weight, bytes_accessed=1, transcendentals=0),
        name="galerkin",
    )(*operands)


def after(value, *others):
    return lax.optimization_barrier((value, *others))[0]


def pause_kernel(value, out):
    out[...] = value[...]


def pause(value):
    return pl.pallas_call(
        pause_kernel,
        out_shape=jax.ShapeDtypeStruct(value.shape, value.dtype),
        cost_estimate=pl.CostEstimate(flops=10**14, bytes_accessed=1, transcendentals=0),
        name="pause",
    )(value)


def shards(a_tiles, a_cols, new_row, p_tiles, p_cols):
    rows = a_tiles.shape[0]
    coarse_rows = rows // 4
    my_x = lax.axis_index("gx").astype(jnp.int32)
    device = my_x * lax.axis_size("gy") + lax.axis_index("gy").astype(jnp.int32)

    operands = (a_cols, new_row, p_tiles, p_cols, my_x.reshape(1))
    send = buckets(["far_a", "d4"], a_tiles, *operands, True)
    p_here = send["p"]
    p_before = beside(p_here, 1)
    p_after = beside(p_here, -1)
    sources = [p_before, p_here, p_after]
    d4 = hop(send["d4"], "gx", 4)
    far_a = hop(send["far_a"], "gx", -6)
    send |= buckets(["far_b", "d3", "d2", "d1", "d0"], after(a_tiles, p_after), *operands, False)
    far_b = hop(after(send["far_b"], p_after), "gx", -6)


    def tables(sources, middle):
        slots = jnp.concatenate([x[-rows:, :P_TILES] for x in sources], axis=0).astype(jnp.int32)
        slots = slots - coarse_rows * device + 4
        return ((middle - 1) * rows).reshape(1), slots, split(sources, rows)

    mine = tables([p_before, p_here, p_after], device)

    def add(data, targets, chunks, befores, weight=1, arrived=None):
        return galerkin(weight, chunks, targets, *data, befores, arrived, rows, coarse_rows)

    d3 = hop(after(send["d3"], p_after), "gx", 3)
    d2 = hop(after(send["d2"], p_before, p_after), "gx", 2)

    both = add(mine, (0, 1), [send["d0"]], None, 10**14)
    far_a = hop(after(far_a, both[0]), "gx", -5)
    p_before_2 = beside(after(p_before, both[0]), 1)
    theirs = tables([p_before_2, p_before, p_here], device - 1)
    d4 = after(d4, both[0])
    both = add(mine, (0, 1), [d4], both, 10**14)
    far_b = hop(after(far_b, both[0]), "gx", -5)
    d1 = hop(after(send["d1"], both[0]), "gx", 1)
    own, on = add(mine, (0, 1), [after(d3, theirs[1], *theirs[2])], both, 10**14)
    token = pause(on[0, :META])
    on = beside(on, 1)
    far_a, d2 = after(far_a, token), after(d2, token)

    f_far_a = beside(far_a, 1)
    f2 = beside(d2, 1)
    (own,) = add(mine, (0,), [d2, far_a], [own], 10**14)
    f1 = beside(after(d1, own), 1)
    f_far_b = beside(after(far_b, own), 1)
    (own,) = add(mine, (0,), [d1, far_b], [own], 10**14)
    (own,) = add(theirs, (0,), [f2, f_far_a, f1, f_far_b], [own], arrived=on)
    return own.reshape(coarse_rows, SLOTS, TILE, TILE)


def solution(mesh):
    in_specs = (
        P(("gx", "gy"), None, None, None),
        P(("gx", "gy"), None),
        P(("gx", "gy")),
        P(("gx", "gy"), None, None, None),
        P(("gx", "gy"), None),
    )
    out_specs = P(("gx", "gy"), None, None, None)
    return jax.shard_map(shards, mesh=mesh, in_specs=in_specs, out_specs=out_specs, check_vma=False)
```

```python
import functools

import jax
import jax.numpy as jnp
from jax import lax
from jax.experimental import pallas as pl
from jax.experimental.pallas import tpu as pltpu
from jax.sharding import PartitionSpec as P

TILE = 128
A_TILES = 4
P_TILES = 2
CAP = 2
SPAN = 6
SLOTS = 10
ROW = A_TILES * TILE
META = 8
WIDTHS = (SLOTS, SLOTS - 2)

BUFFERS = {
    "far_a": (((10, 0, ROW),), True),
    "far_b": (((11, 0, ROW),), True),
    "d4": (((8, 0, ROW), (9, 0, ROW)), True),
    "d3": (((6, 0, ROW), (7, 0, ROW)), True),
    "d2": (((4, 0, ROW), (5, 0, ROW)), True),
    "d1": (((2, 0, ROW), (3, 0, ROW)), True),
    "d0": (((0, 0, ROW), (1, 0, ROW)), True),
}

ANY = pl.BlockSpec(memory_space=pl.ANY)
HBM = pl.BlockSpec(memory_space=pltpu.MemorySpace.HBM)
SMEM = pl.BlockSpec(memory_space=pltpu.SMEM)
VMEM = pl.BlockSpec(memory_space=pltpu.VMEM)


def hop(value, axis, steps):
    count = lax.axis_size(axis)
    return lax.ppermute(value, axis, [(i, (i + steps) % count) for i in range(count)])


def beside(value, steps):
    count = lax.axis_size("gy")
    route = [(i, i + steps) for i in range(count) if 0 <= i + steps < count]
    return lax.ppermute(value, "gy", route)


def bucket_kernel(rows, gx, per_x, layout, first, new_row, a_cols, p_cols, my_x, a_hbm, p_hbm, *refs):
    if first:
        p_out, refs = refs[0], refs[1:]
    outs, refs = refs[: len(layout)], refs[len(layout) :]
    held, held_p, notes, order, in_sem, out_sem, note_sem, p_sem = refs
    p_size = rows * P_TILES * TILE
    if first:
        p_load = pltpu.make_async_copy(p_hbm, held_p.at[pl.ds(0, p_size)], p_sem)
    loads = [pltpu.make_async_copy(a_hbm.at[o], held.at[o], in_sem.at[o]) for o in range(rows)]
    for s in range(SPAN * CAP):
        order[s] = -1
    gaps = [lax.rem(lax.div(new_row[o], per_x) - my_x[0] + gx, gx) for o in range(rows)]
    for o in range(rows):
        rank = sum([(gaps[e] == gaps[o]).astype(jnp.int32) for e in range(o)], jnp.int32(0))
        order[gaps[o] * CAP + rank] = o
    places = [s for pieces, _ in layout for s, _, _ in pieces]

    def wanted(o):
        return sum([(order[s] == o).astype(jnp.int32) for s in places]) > 0

    for o, load in enumerate(loads):

        @pl.when(wanted(o))
        def _():
            load.start()

    if first:
        p_load.start()
    lane = lax.broadcasted_iota(jnp.int32, (META, TILE), 1)
    line = lax.broadcasted_iota(jnp.int32, (META, TILE), 0)
    note_copies = []
    for b, (pieces, noted) in enumerate(layout):
        if not noted:
            continue
        note = jnp.zeros((META, TILE), jnp.int32)
        for r, (s, _, _) in enumerate(pieces):
            o = order[s]
            here = jnp.maximum(o, 0)
            place = jnp.where(o >= 0, lax.rem(new_row[here], rows) + 1, 0)
            for k in range(A_TILES):
                note = jnp.where((line == r) & (lane == k), a_cols[k, here], note)
            note = jnp.where((line == r) & (lane == A_TILES), place, note)
        notes[b] = note.astype(jnp.float32)
        size = sum(n for _, _, n in pieces)
        copy = pltpu.make_async_copy(notes.at[b], outs[b].at[pl.ds(size, META)], note_sem.at[b])
        copy.start()
        note_copies.append(copy)
    if first:
        note = jnp.zeros((META, TILE), jnp.int32)
        for i in range(rows):
            for q in range(P_TILES):
                note = jnp.where((line == i) & (lane == q), p_cols[q, i], note)
        held_p[p_size:, :] = note.astype(jnp.float32)
    for o, load in enumerate(loads):

        @pl.when(wanted(o))
        def _():
            load.wait()

    def each(act):
        n = 0
        for out, (pieces, _) in zip(outs, layout):
            to = 0
            for s, frm, size in pieces:
                o = order[s]
                here = jnp.maximum(o, 0)

                @pl.when(o >= 0)
                def _():
                    act(
                        pltpu.make_async_copy(
                            held.at[here, pl.ds(frm, size)], out.at[pl.ds(to, size)], out_sem.at[n]
                        )
                    )

                to += size
                n += 1

    each(lambda copy: copy.start())
    if first:
        p_load.wait()
        p_copy = pltpu.make_async_copy(held_p, p_out, p_sem)
        p_copy.start()
    each(lambda copy: copy.wait())
    for copy in note_copies:
        copy.wait()
    if first:
        p_copy.wait()


def buckets(names, a_tiles, a_cols, new_row, p_tiles, p_cols, my_x, first):
    rows = a_tiles.shape[0]
    gx, gy = lax.axis_size("gx"), lax.axis_size("gy")
    layout = [BUFFERS[name] for name in names]
    lengths = [sum(n for _, _, n in pieces) + META * noted for pieces, noted in layout]
    p_lines = rows * P_TILES * TILE
    outs = pl.pallas_call(
        functools.partial(bucket_kernel, rows, gx, rows * gy, layout, first),
        out_shape=[jax.ShapeDtypeStruct((n, TILE), jnp.float32) for n in [p_lines + META] * first + lengths],
        in_specs=[SMEM, SMEM, SMEM, SMEM, HBM, HBM],
        out_specs=[HBM] * (first + len(lengths)),
        scratch_shapes=[
            pltpu.VMEM((rows, ROW, TILE), jnp.float32),
            pltpu.VMEM((p_lines + META, TILE), jnp.float32),
            pltpu.VMEM((len(lengths), META, TILE), jnp.float32),
            pltpu.SMEM((SPAN * CAP,), jnp.int32),
            pltpu.SemaphoreType.DMA((rows,)),
            pltpu.SemaphoreType.DMA((sum(len(p) for p, _ in layout),)),
            pltpu.SemaphoreType.DMA((len(lengths),)),
            pltpu.SemaphoreType.DMA,
        ],
        compiler_params=pltpu.CompilerParams(vmem_limit_bytes=60 * 2**20),
        name="buckets",
    )(new_row, a_cols.T, p_cols.T, my_x, a_tiles.reshape(rows, ROW, TILE), p_tiles.reshape(p_lines, TILE))
    return dict(zip(["p"] * first + names, outs))


def halves(x):
    high = x.astype(jnp.bfloat16)
    return high, (x - high.astype(jnp.float32)).astype(jnp.bfloat16)


def split_kernel(rows, *refs):
    sources, (high, low, turned) = refs[:3], refs[3:]
    for n, source in enumerate(sources):

        def body(i, carry):
            for q in range(P_TILES):
                block = source[pl.ds(pl.multiple_of((i * P_TILES + q) * TILE, TILE), TILE), :]
                h, l = halves(block)
                high[n * rows + i, :, q * TILE : (q + 1) * TILE] = h
                low[n * rows + i, :, q * TILE : (q + 1) * TILE] = l
                if n == 1:
                    h, l = halves(block.T)
                    turned[i * P_TILES + q, :TILE, :] = h
                    turned[i * P_TILES + q, TILE:, :] = l
            return carry

        lax.fori_loop(0, rows, body, 0)


def split(sources, rows):
    wide = jax.ShapeDtypeStruct((3 * rows, TILE, P_TILES * TILE), jnp.bfloat16)
    return pl.pallas_call(
        functools.partial(split_kernel, rows),
        out_shape=[wide, wide, jax.ShapeDtypeStruct((rows * P_TILES, 2 * TILE, TILE), jnp.bfloat16)],
        in_specs=[VMEM] * 3,
        out_specs=[VMEM] * 3,
        compiler_params=pltpu.CompilerParams(vmem_limit_bytes=12 * 2**20),
        name="split",
    )(*sources)


def galerkin_kernel(rows, chunks, targets, fresh, joined, slots, first, high, low, turned, *refs):
    buffers, refs = refs[: len(chunks)], refs[len(chunks) :]
    if not fresh:
        befores, refs = refs[: len(targets)], refs[len(targets) :]
    if joined:
        arrived, refs = refs[0], refs[1:]
    accs, refs = refs[: len(targets)], refs[len(targets) :]
    lifted, held, notes, note_sem, sem = refs
    note_copies, lines = [], []
    for n, (buffer, length) in enumerate(zip(buffers, chunks)):
        copy = pltpu.make_async_copy(buffer.at[pl.ds(length - META, META)], notes.at[n], note_sem.at[n])
        copy.start()
        note_copies.append(copy)
        lines += [(n, r) for r in range(length // ROW)]
    def fetch(m):
        n, r = lines[m]
        return pltpu.make_async_copy(buffers[n].at[pl.ds(r * ROW, ROW)], held.at[m], sem.at[m])

    for m in range(len(lines)):
        fetch(m).start()
    for i, acc in enumerate(accs):
        if fresh:
            acc[...] = jnp.zeros_like(acc)
        else:
            acc[...] = befores[i][...]
    if joined:
        for i in range(arrived.shape[0] // WIDTHS[1]):
            to = i * SLOTS
            acc[to : to + WIDTHS[1]] += arrived[i * WIDTHS[1] : (i + 1) * WIDTHS[1]]
    for copy in note_copies:
        copy.wait()

    def note(n, r, k):
        return notes[n, r, k].astype(jnp.int32)

    for m, (n, r) in enumerate(lines):

        fetch(m).wait()

        @pl.when(note(n, r, A_TILES) > 0)
        def _():
            row = note(n, r, A_TILES) - 1
            cols = [note(n, r, k) - first[0] for k in range(A_TILES)]
            for k, c in enumerate(cols):
                h, l = halves(held[m, k * TILE : (k + 1) * TILE, :])
                left = jnp.concatenate([h, l], axis=1)
                t = jnp.dot(
                    left, jnp.concatenate([high[c], high[c]], axis=0), preferred_element_type=jnp.float32
                ) + jnp.dot(
                    left, jnp.concatenate([low[c], low[c]], axis=0), preferred_element_type=jnp.float32
                )
                h, l = halves(t)
                span = slice(k * P_TILES * TILE, (k + 1) * P_TILES * TILE)
                lifted[:TILE, span] = h
                lifted[TILE:, span] = l
            for p in range(P_TILES):
                for target, acc in zip(targets, accs):
                    mine = slots[rows + row, p] - 4 - 2 * target

                    @pl.when((mine == 0) | (mine == 1))
                    def _():
                        left = turned[row * P_TILES + p]
                        w = jnp.dot(
                            jnp.concatenate([left, left], axis=1), lifted[...], preferred_element_type=jnp.float32
                        )
                        w = w[:TILE] + w[TILE:]
                        for k, c in enumerate(cols):
                            for q in range(P_TILES):
                                lanes = (k * P_TILES + q) * TILE
                                s = mine * WIDTHS[target] + slots[c, q] - 2 * target
                                acc[s] += w[:, lanes : lanes + TILE]


def galerkin(weight, chunks, targets, first_row, slots, splits, befores, arrived, rows, coarse_rows):
    shapes = [x.shape[0] for x in chunks]
    out = [jax.ShapeDtypeStruct((coarse_rows * WIDTHS[t], TILE, TILE), jnp.float32) for t in targets]
    befores, joined = list(befores or []), [] if arrived is None else [arrived]
    operands = [slots, first_row, *splits, *chunks, *befores, *joined]
    specs = [SMEM, SMEM] + [VMEM] * len(splits) + [ANY] * len(chunks) + [VMEM] * len(befores + joined)
    lines = sum(n // ROW for n in shapes)
    return pl.pallas_call(
        functools.partial(galerkin_kernel, rows, shapes, targets, not befores, bool(joined)),
        out_shape=out,
        in_specs=specs,
        out_specs=[VMEM] * len(out),
        scratch_shapes=[
            pltpu.VMEM((2 * TILE, A_TILES * P_TILES * TILE), jnp.bfloat16),
            pltpu.VMEM((lines, ROW, TILE), jnp.float32),
            pltpu.SMEM((len(chunks), META, TILE), jnp.float32),
            pltpu.SemaphoreType.DMA((len(chunks),)),
            pltpu.SemaphoreType.DMA((lines,)),
        ],
        compiler_params=pltpu.CompilerParams(vmem_limit_bytes=20 * 2**20),
        cost_estimate=pl.CostEstimate(flops=weight, bytes_accessed=1, transcendentals=0),
        name="galerkin",
    )(*operands)


def after(value, *others):
    return lax.optimization_barrier((value, *others))[0]


def pause_kernel(value, out):
    out[...] = value[...]


def pause(value):
    return pl.pallas_call(
        pause_kernel,
        out_shape=jax.ShapeDtypeStruct(value.shape, value.dtype),
        cost_estimate=pl.CostEstimate(flops=10**14, bytes_accessed=1, transcendentals=0),
        name="pause",
    )(value)


def shards(a_tiles, a_cols, new_row, p_tiles, p_cols):
    rows = a_tiles.shape[0]
    coarse_rows = rows // 4
    my_x = lax.axis_index("gx").astype(jnp.int32)
    device = my_x * lax.axis_size("gy") + lax.axis_index("gy").astype(jnp.int32)

    operands = (a_cols, new_row, p_tiles, p_cols, my_x.reshape(1))
    send = buckets(["far_a", "d4"], a_tiles, *operands, True)
    p_here = send["p"]
    p_before = beside(p_here, 1)
    p_after = beside(p_here, -1)
    sources = [p_before, p_here, p_after]
    d4 = hop(send["d4"], "gx", 4)
    far_a = hop(send["far_a"], "gx", -6)
    send |= buckets(["far_b", "d3", "d2", "d1", "d0"], after(a_tiles, p_after), *operands, False)
    far_b = hop(after(send["far_b"], p_after), "gx", -6)


    def tables(sources, middle):
        slots = jnp.concatenate([x[-rows:, :P_TILES] for x in sources], axis=0).astype(jnp.int32)
        slots = slots - coarse_rows * device + 4
        return ((middle - 1) * rows).reshape(1), slots, split(sources, rows)

    mine = tables([p_before, p_here, p_after], device)

    def add(data, targets, chunks, befores, weight=1, arrived=None):
        return galerkin(weight, chunks, targets, *data, befores, arrived, rows, coarse_rows)

    d3 = hop(after(send["d3"], p_after), "gx", 3)
    d2 = hop(after(send["d2"], p_before, p_after), "gx", 2)

    both = add(mine, (0, 1), [send["d0"]], None, 10**14)
    far_a = hop(after(far_a, both[0]), "gx", -5)
    p_before_2 = beside(after(p_before, both[0]), 1)
    theirs = tables([p_before_2, p_before, p_here], device - 1)
    d4 = after(d4, both[0])
    both = add(mine, (0, 1), [d4], both, 10**14)
    far_b = hop(after(far_b, both[0]), "gx", -5)
    d1 = hop(after(send["d1"], both[0]), "gx", 1)
    own, on = add(mine, (0, 1), [after(d3, theirs[1], *theirs[2])], both, 10**14)
    token = pause(on[0, :META])
    on = beside(on, 1)
    far_a, d2 = after(far_a, token), after(d2, token)

    f_far_a = beside(far_a, 1)
    f2 = beside(d2, 1)
    (own,) = add(mine, (0,), [d2, far_a], [own], 10**14)
    mid = own
    token = pause(mid[0, :META])
    far_b = after(far_b, token)
    (own,) = add(theirs, (0,), [after(f2, token), f_far_a], [own], arrived=on)
    f1 = beside(after(d1, mid), 1)
    f_far_b = beside(far_b, 1)
    (own,) = add(mine, (0,), [d1, far_b], [own], 10**14)
    (own,) = add(theirs, (0,), [f1, f_far_b], [own])
    return own.reshape(coarse_rows, SLOTS, TILE, TILE)


def solution(mesh):
    in_specs = (
        P(("gx", "gy"), None, None, None),
        P(("gx", "gy"), None),
        P(("gx", "gy")),
        P(("gx", "gy"), None, None, None),
        P(("gx", "gy"), None),
    )
    out_specs = P(("gx", "gy"), None, None, None)
    return jax.shard_map(shards, mesh=mesh, in_specs=in_specs, out_specs=out_specs, check_vma=False)
```
